512 devices in a mesh: ctx: 128 (over z, y, core), tp: 4 (over x).
Axes of the slice: x: 4, y: 8, z: 8, core: 2. Of those that a mesh axis runs over, the one named last changes fastest.
Arguments:
- query: bfloat16 [32768, 4096], P('ctx', 'tp'), may hold values from -96 to 96
- key: bfloat16 [32768, 4096], P('ctx', 'tp'), may hold values from -4 to 4
- value: bfloat16 [32768, 4096], P('ctx', 'tp'), may hold values from -6 to 6
- xin: bfloat16 [32768, 4096], P('ctx', 'tp'), may hold values from -1 to 8
- gate_z: bfloat16 [32768, 4096], P('ctx', 'tp'), may hold values from -6 to 6
- w_bc: bfloat16 [4096, 32], P('tp'), may hold values from -1 to 1
- dt_low: bfloat16 [32768, 256], P('ctx'), may hold values from -4 to 9
- dt_proj: bfloat16 [256, 4096], P(None, 'tp'), may hold values from -3 to 3
- dt_bias: float32 [4096], P('tp'), may hold values from -20 to 0
- a_rate: float32 [16, 4096], P(None, 'tp'), may hold values from 1 to 16
- skip: float32 [4096], P('tp'), may hold values from 0.2 to 2
Outputs:
- attended: bfloat16 [32768, 4096], P('ctx', 'tp')
- mixed: bfloat16 [32768, 4096], P('ctx', 'tp')
The draws below stay inside these ranges and needn't reach their ends.
All inputs are finite; a program needn't handle non-finite values.
Results may differ from the reference program's by a relative error of at most 0.0085.
Values may be sent and summed in bfloat16 or wider, within the bound.
No kernel may reach another device: no remote copies, remote signals or barrier semaphores. Data moves between devices by JAX's collectives and lax.ppermute only.
A program may use at most 128 MiB of HBM per device.

```python
import math
import jax
import jax.numpy as jnp
from jax import lax

HEADS = 32
HD = 128
WINDOW = 2048
CH = 4096
NS = 16
DT_RANK = 256
TOK_DEV = 256
STRING_LENGTH = 32768


def drawn_rows(key):
    key_rows = jnp.clip(jax.random.normal(jax.random.fold_in(key, 101), (STRING_LENGTH, HEADS * HD), jnp.float32), -4.0, 4.0)
    return key_rows


def draw_key(key, part):
    key_rows = drawn_rows(key)
    return key_rows.astype(jnp.bfloat16)


def draw_query(key, part):
    queries = 2.5 * jnp.clip(jax.random.normal(jax.random.fold_in(key, 103), (STRING_LENGTH, HEADS * HD), jnp.float32), -6.0, 6.0)
    return queries.astype(jnp.bfloat16)


def draw_xin(key, part):
    raw_vals = 2.0 * jnp.clip(jax.random.normal(jax.random.fold_in(key, 201), (STRING_LENGTH, CH), jnp.float32), -4.0, 4.0)
    return jax.nn.silu(raw_vals).astype(jnp.bfloat16)


def draw_w_bc(key, part):
    base_vals = jnp.clip(jax.random.normal(jax.random.fold_in(key, 301), (CH, 2 * NS), jnp.float32), -6.0, 6.0) / math.sqrt(CH)
    signs = jnp.where(jax.random.bernoulli(jax.random.fold_in(key, 302), 0.5, (NS,)), 1.0, -1.0)
    magnitude = jax.random.uniform(jax.random.fold_in(key, 303), (NS,), jnp.float32, 0.5, 1.5)
    offsets = jnp.concatenate([signs * magnitude * 2.0 / CH, jnp.zeros((NS,), jnp.float32)])
    return (base_vals + offsets[None, :]).astype(jnp.bfloat16)


def draw_dt_low(key, part):
    entry_indices = jnp.arange(STRING_LENGTH)
    packet_bundles = jax.random.randint(jax.random.fold_in(key, 401), (8,), 0, STRING_LENGTH)
    packet_slot = jnp.where(jnp.any(entry_indices[:, None] == packet_bundles[None, :], axis=1), 9.0, 0.0)
    block_vals = jax.random.uniform(jax.random.fold_in(key, 402), (STRING_LENGTH // TOK_DEV,), jnp.float32, -1.0, 1.0)
    worker_slot = block_vals[entry_indices // TOK_DEV]
    leftover_entries = jnp.clip(jax.random.normal(jax.random.fold_in(key, 403), (STRING_LENGTH, DT_RANK - 2), jnp.float32), -4.0, 4.0)
    merged_result = jnp.concatenate([packet_slot[:, None], worker_slot[:, None], leftover_entries], axis=1)
    return merged_result.astype(jnp.bfloat16)


def draw_dt_proj(key, part):
    first_row = jax.random.uniform(jax.random.fold_in(key, 501), (1, CH), jnp.float32, 0.95, 1.05)
    second_row = jax.random.uniform(jax.random.fold_in(key, 502), (1, CH), jnp.float32, -0.8, 0.8)
    leftover_entries = jnp.clip(jax.random.normal(jax.random.fold_in(key, 503), (DT_RANK - 2, CH), jnp.float32), -4.0, 4.0) * (0.6 / math.sqrt(DT_RANK - 2))
    return jnp.concatenate([first_row, second_row, leftover_entries], axis=0).astype(jnp.bfloat16)


def draw_dt_bias(key, part):
    slow_share = 0.5
    chooser = jax.random.uniform(jax.random.fold_in(key, 601), (CH,), jnp.float32)
    slow_vals = -jnp.log(jax.random.uniform(jax.random.fold_in(key, 602), (CH,), jnp.float32, 2.0, 6.0) * STRING_LENGTH)
    fast_vals = -jax.random.uniform(jax.random.fold_in(key, 603), (CH,), jnp.float32, math.log(24.0), math.log(max(48.0, 2.0 * TOK_DEV)))
    return jnp.where(chooser < slow_share, slow_vals, fast_vals).astype(jnp.float32)


def level_of(stream_key, extent, shards, least, largest):
    factor_of = 1.0
    for axis_at, shards_of in shards:
        steps = jax.random.uniform(jax.random.fold_in(jax.random.fold_in(stream_key, 6), axis_at), (shards_of,), jnp.float32, least / len(shards), largest / len(shards))
        factor_of = factor_of * jnp.repeat(jnp.exp(steps), extent[axis_at] // shards_of).reshape((-1,) + (1,) * (len(extent) - 1 - axis_at))
    return factor_of


def noise(own_key, dims, scale, most, pieces=(), kind=jnp.bfloat16):
    array = jax.random.normal(own_key, dims, jnp.float32) * scale
    if len(pieces) > 0:
        array = level_of(own_key, dims, pieces, -0.22, 0.18) * array
    return jnp.clip(array, min=-most, max=most).astype(kind)


def setup_inputs(seed: int = 0) -> dict:
    keys = jax.random.split(jax.random.key(seed), 12)
    return {
        "query": draw_query(jax.random.fold_in(keys[11], 71), 0),
        "key": draw_key(jax.random.fold_in(keys[11], 71), 0),
        "value": noise(keys[2], (STRING_LENGTH, HEADS * HD), 1.0, 6.0, ((0, 128), (1, 4))),
        "xin": draw_xin(jax.random.fold_in(keys[11], 71), 0),
        "gate_z": noise(keys[4], (STRING_LENGTH, CH), 1.0, 6.0, ((0, 128), (1, 4))),
        "w_bc": draw_w_bc(jax.random.fold_in(keys[11], 71), 0),
        "dt_low": draw_dt_low(jax.random.fold_in(keys[11], 71), 0),
        "dt_proj": draw_dt_proj(jax.random.fold_in(keys[11], 71), 0),
        "dt_bias": draw_dt_bias(jax.random.fold_in(keys[11], 71), 0),
        "a_rate": jnp.clip(jnp.exp(math.log(16.0) - 2.7725887 * jax.random.uniform(keys[9], (NS, CH), jnp.float32) ** level_of(keys[9], (NS, CH), ((1, 4),), -0.2, 0.2)), 1.0, 16.0),
        "skip": jnp.clip(jnp.exp(math.log(2.0) - 2.3025851 * jax.random.uniform(keys[10], (CH,), jnp.float32) ** level_of(keys[10], (CH,), ((0, 4),), -0.2, 0.2)), 0.2, 2.0),
    }


def attention_part(query, key, value):
    block_len = TOK_DEV
    padding = jnp.zeros((WINDOW, HEADS * HD), jnp.bfloat16)
    key_padded = jnp.concatenate([padding, key], axis=0)
    value_padded = jnp.concatenate([padding, value], axis=0)
    scale = HD ** -0.5

    def one_block(block_id):
        start = (block_id * block_len).astype(jnp.int32)
        q_rows = lax.dynamic_slice_in_dim(query, start, block_len, 0).reshape(block_len, HEADS, HD).astype(jnp.float32)
        k_rows = lax.dynamic_slice_in_dim(key_padded, start, WINDOW + block_len, 0).reshape(WINDOW + block_len, HEADS, HD).astype(jnp.float32)
        v_rows = lax.dynamic_slice_in_dim(value_padded, start, WINDOW + block_len, 0).reshape(WINDOW + block_len, HEADS, HD).astype(jnp.float32)
        scores = jnp.einsum("qhd,khd->hqk", q_rows, k_rows) * scale
        query_pos = start + jnp.arange(block_len, dtype=jnp.int32)
        key_pos = start - WINDOW + jnp.arange(WINDOW + block_len, dtype=jnp.int32)
        allowed = (key_pos[None, :] <= query_pos[:, None]) & (key_pos[None, :] > query_pos[:, None] - WINDOW) & (key_pos[None, :] >= 0)
        masked = jnp.where(allowed[None], scores, -jnp.inf)
        row_max = jnp.max(masked, axis=2, keepdims=True)
        unscaled = jnp.where(allowed[None], jnp.exp(scores - row_max), 0.0)
        row_sum = jnp.sum(unscaled, axis=2, keepdims=True)
        probs = (unscaled / row_sum).astype(jnp.bfloat16)
        output = jnp.einsum("hqk,khd->qhd", probs.astype(jnp.float32), v_rows)
        return output.reshape(block_len, HEADS * HD).astype(jnp.bfloat16)

    blocks = lax.map(one_block, jnp.arange(STRING_LENGTH // block_len, dtype=jnp.int32))
    return blocks.reshape(STRING_LENGTH, HEADS * HD)


def reference(query, key, value, xin, gate_z, w_bc, dt_low, dt_proj, dt_bias, a_rate, skip):
    attended = attention_part(query, key, value)
    summed_bc = jnp.dot(xin, w_bc, preferred_element_type=jnp.float32)
    b_rows = summed_bc[:, :NS]
    c_rows = summed_bc[:, NS:]
    step_sizes = jax.nn.softplus(jnp.dot(dt_low, dt_proj, preferred_element_type=jnp.float32) + dt_bias[None, :])

    def advance(carried, inputs):
        step_row, input_row, b_vec, c_vec, gate_row = inputs
        input_f = input_row.astype(jnp.float32)
        driven = step_row * input_f
        carried = jnp.exp(-step_row[None, :] * a_rate) * carried + driven[None, :] * b_vec[:, None]
        output = jnp.sum(c_vec[:, None] * carried, axis=0) + skip * input_f
        gated = output * jax.nn.silu(gate_row.astype(jnp.float32))
        return carried, gated.astype(jnp.bfloat16)

    start_state = jnp.zeros((NS, CH), jnp.float32)
    last_state, mixed = lax.scan(advance, start_state, (step_sizes, xin, b_rows, c_rows, gate_z))
    return attended, mixed
```

```python
import jax
import jax.numpy as jnp
from jax import lax
from jax.experimental import pallas as pl
from jax.experimental.pallas import tpu as pltpu
from jax.sharding import PartitionSpec as P


HD = 128
WINDOW = 2048
NS = 16
LANES = 128
TILES = 8
LOG2E = 1.4426950408889634
F32 = jnp.float32
BF16 = jnp.bfloat16
VMEM = pl.BlockSpec(memory_space=pltpu.VMEM)
SMEM = pl.BlockSpec(memory_space=pltpu.SMEM)


def cost(flops, moved, exps=0):
    return pl.CostEstimate(flops=flops, bytes_accessed=moved, transcendentals=exps)


def local(body, outs, scratch=(), scalars=0, arrays=1, estimate=None, limit=48 << 20):
    return pl.pallas_call(
        body,
        out_shape=outs,
        in_specs=[SMEM] * scalars + [VMEM] * arrays,
        out_specs=jax.tree.map(lambda _: VMEM, outs),
        scratch_shapes=list(scratch),
        cost_estimate=estimate,
        compiler_params=pltpu.CompilerParams(vmem_limit_bytes=limit),
    )


def parity_of(place):
    return place[0] & 1


def plane_of(place):
    return place[0] >> 4


def pack_body(*refs):
    *ins, out = refs
    rows = ins[0].shape[0]
    for head in range(out.shape[0]):
        for k, part in enumerate(ins):
            out[head, k * rows : (k + 1) * rows, :] = part[:, head * HD : (head + 1) * HD]


def pack(*parts):
    rows, width = parts[0].shape
    out = jax.ShapeDtypeStruct((width // HD, len(parts) * rows, HD), BF16)
    moved = 4 * len(parts) * rows * width
    return local(pack_body, out, arrays=len(parts), estimate=cost(0, moved))(*parts)


def unpack_body(blocks, out):
    for head in range(blocks.shape[0]):
        out[:, head * HD : (head + 1) * HD] = blocks[head]


def unpack(blocks):
    heads, rows, _ = blocks.shape
    out = jax.ShapeDtypeStruct((rows, heads * HD), BF16)
    return local(unpack_body, out, estimate=cost(0, 4 * rows * heads * HD))(blocks)


def attend_body(place, queries, own, other, old, past, out, ko, vo, kp, vp):
    blocks, rows, _ = queries.shape
    half = old.shape[0]
    parity = parity_of(place)
    live = plane_of(place) > 0
    key0 = jnp.where(parity == 0, own[0, 0:1, :].astype(F32), other[0, 0:1, :].astype(F32))
    key0 = jnp.broadcast_to(key0, (rows, HD)).astype(BF16)
    ones = jnp.ones((rows, HD), BF16)
    shown = jnp.where(live, jnp.ones((rows, HD), F32), jnp.zeros((rows, HD), F32)).astype(BF16)
    for keys, values, source in ((ko, vo, old), (kp, vp, past)):
        for b in range(half):
            at = slice(b * rows, (b + 1) * rows)
            values[at, 0:HD] = source[b, rows : 2 * rows, :]
            values[at, HD : 2 * HD] = shown

        @pl.when(live)
        def _():
            for b in range(half):
                keys[b * rows : (b + 1) * rows, :] = source[b, 0:rows, :]

        @pl.when(jnp.logical_not(live))
        def _():
            for b in range(half):
                keys[b * rows : (b + 1) * rows, :] = key0

    for keys, values, source in ((ko, vo, own), (kp, vp, other)):
        for b in range(blocks):
            at = slice((half + b) * rows, (half + b + 1) * rows)
            keys[at, :] = source[b, 0:rows, :]
            values[at, 0:HD] = source[b, rows : 2 * rows, :]
            values[at, HD : 2 * HD] = ones
    scale = HD**-0.5 * LOG2E
    columns = lax.broadcasted_iota(jnp.int32, (rows, rows), 1)
    below = columns <= lax.broadcasted_iota(jnp.int32, (rows, rows), 0)

    def dots(q, k):
        return lax.dot_general(q, k, (((1,), (1,)), ((), ())), preferred_element_type=F32)

    def span(block, count):
        return pl.ds(pl.multiple_of(block * rows, rows), count * rows)

    def one(i, carry):
        q = queries[i]
        edge = jnp.where(below, dots(q, ko[span(i + half, 1), :]), dots(q, ko[span(i, 1), :]))
        mid = dots(q, ko[span(i + 1, half - 1), :])
        par = dots(q, kp[span(i + parity, half), :])
        top = None
        for part in (edge, mid, par):
            for c in range(0, part.shape[1], LANES):
                piece = part[:, c : c + LANES]
                top = piece if top is None else jnp.maximum(top, piece)
        top = jnp.max(top, axis=1, keepdims=True) * scale
        weight = jnp.exp2(edge * scale - top)
        near = jnp.where(below, weight, 0.0).astype(BF16)
        far = jnp.where(below, 0.0, weight).astype(BF16)
        w_mid = jnp.exp2(mid * scale - top).astype(BF16)
        w_par = jnp.exp2(par * scale - top).astype(BF16)
        total = jnp.dot(w_mid, vo[span(i + 1, half - 1), :], preferred_element_type=F32)
        total += jnp.dot(w_par, vp[span(i + parity, half), :], preferred_element_type=F32)
        total += jnp.dot(near, vo[span(i + half, 1), :], preferred_element_type=F32)
        total += jnp.dot(far, vo[span(i, 1), :], preferred_element_type=F32)
        out[i] = (total[:, 0:HD] / total[:, HD : 2 * HD]).astype(BF16)
        return carry

    lax.fori_loop(0, blocks, one, 0, unroll=2)


def attend(place, queries, own, other, old, past):
    blocks, rows, _ = queries.shape
    ext = (blocks + old.shape[0]) * rows
    scratch = [pltpu.VMEM((ext, HD), BF16), pltpu.VMEM((ext, 2 * HD), BF16)] * 2
    out = jax.ShapeDtypeStruct(queries.shape, BF16)
    estimate = cost(4 * blocks * rows * WINDOW * 2 * HD, 8 << 20, blocks * rows * WINDOW)
    return local(attend_body, out, scratch, 1, 5, estimate)(place, queries, own, other, old, past)


def rows_of(step):
    return pl.ds(pl.multiple_of(step * TILES, TILES), TILES)


def project_body(xin, w_bc, out):
    out[...] = jnp.dot(xin[...], w_bc[...], preferred_element_type=F32).T


def project(xin, w_bc):
    out = jax.ShapeDtypeStruct((w_bc.shape[1], xin.shape[0]), F32)
    return local(project_body, out, arrays=2, estimate=cost(0, 2 * xin.size))(xin, w_bc)


def steps_body(low, proj, bias, xin, steps, drive):
    rows = low.shape[0]
    for c in range(TILES):
        col = slice(c * LANES, (c + 1) * LANES)
        raw = jnp.dot(low[...], proj[:, col], preferred_element_type=F32) + bias[:, col]
        size = jnp.maximum(raw, 0.0) + jnp.log1p(jnp.exp(-jnp.abs(raw)))
        steps[pl.ds(c, rows, stride=TILES), :] = size
        drive[pl.ds(c, rows, stride=TILES), :] = size * xin[:, col].astype(F32)


def step_sizes(low, proj, bias, xin):
    rows, width = xin.shape
    out = jax.ShapeDtypeStruct((rows * TILES, LANES), F32)
    estimate = cost(2 * rows * low.shape[1] * width, 12 * rows * width, 2 * rows * width)
    return local(steps_body, (out, out), arrays=4, estimate=estimate)(
        low, proj, bias.reshape(1, -1), xin
    )


def spread(parts, count, wide):
    total = parts[0][0:count, :]
    for part in parts[1:]:
        total = total + part[0:count, :]
    total = total.T
    rows = total.shape[0]
    for n in range(count):
        column = jnp.broadcast_to(total[:, n : n + 1], (rows, LANES))
        wide[pl.ds(n, rows, stride=count), :] = column


def load_rates(a_rate, held):
    for c in range(TILES):
        held[pl.ds(c, NS, stride=TILES), :] = a_rate[:, c * LANES : (c + 1) * LANES] * -LOG2E
    return [held[n * TILES : (n + 1) * TILES, :] for n in range(NS)]


def ends_body(steps, drive, p0, p1, p2, p3, a_rate, out, held, wide):
    rows = p0.shape[1]
    spread((p0, p1, p2, p3), NS, wide)
    rates = load_rates(a_rate, held)

    def step(t, carry):
        state, through = carry
        size, push = steps[rows_of(t), :], drive[rows_of(t), :]
        state = tuple(
            jnp.exp2(size * rates[n]) * state[n] + push * wide[pl.ds(t * NS + n, 1), :]
            for n in range(NS)
        )
        return state, through + size

    zero = jnp.zeros((TILES, LANES), F32)
    state, through = lax.fori_loop(0, rows, step, ((zero,) * NS, zero), unroll=4)
    for n in range(NS):
        out[n * TILES : (n + 1) * TILES, :] = state[n]
    out[NS * TILES :, :] = through


def block_ends(steps, drive, partials, a_rate):
    rows = partials[0].shape[1]
    out = jax.ShapeDtypeStruct(((NS + 1) * TILES, LANES), F32)
    rates = jax.ShapeDtypeStruct((NS * TILES, LANES), F32)
    scratch = [pltpu.VMEM((rows * NS, LANES), F32)]
    estimate = cost(6 * steps.size * NS, 8 * steps.size, steps.size * NS)
    return local(ends_body, (out, rates), scratch, 0, 7, estimate)(steps, drive, *partials, a_rate)


def fold(rates, parts):
    state = [parts[0][n * TILES : (n + 1) * TILES, :] for n in range(NS)]
    through = parts[0][NS * TILES :, :]
    for part in parts[1:]:
        size = part[NS * TILES :, :]
        for n in range(NS):
            row = slice(n * TILES, (n + 1) * TILES)
            state[n] = jnp.exp2(size * rates[row, :]) * state[n] + part[row, :]
        through = through + size
    return state, through


def join_body(rates, *refs):
    *parts, out = refs
    state, through = fold(rates, parts)
    for n in range(NS):
        out[n * TILES : (n + 1) * TILES, :] = state[n]
    out[NS * TILES :, :] = through


def join(rates, parts):
    out = jax.ShapeDtypeStruct(parts[0].shape, F32)
    estimate = cost(1 << 16, 1 << 18)
    return local(join_body, out, arrays=1 + len(parts), estimate=estimate)(rates, *parts)


def final_body(steps, drive, p0, p1, p2, p3, held, e0, e1, e2, e3, xin, gate, skip, out, wide, mix):
    rows = p0.shape[1]
    spread((p0, p1, p2, p3), 2 * NS, wide)
    rates = [held[n * TILES : (n + 1) * TILES, :] for n in range(NS)]
    state, _ = fold(held, (e0, e1, e2, e3))

    def step(t, state):
        size, push = steps[rows_of(t), :], drive[rows_of(t), :]
        after = []
        result = None
        for n in range(NS):
            at = t * 2 * NS + n
            now = jnp.exp2(size * rates[n]) * state[n] + push * wide[pl.ds(at, 1), :]
            after.append(now)
            term = now * wide[pl.ds(at + NS, 1), :]
            result = term if result is None else result + term
        mix[rows_of(t), :] = result
        return tuple(after)

    lax.fori_loop(0, rows, step, tuple(state), unroll=4)
    for c in range(TILES):
        col = slice(c * LANES, (c + 1) * LANES)
        mixed = mix[pl.ds(c, rows, stride=TILES), :] + skip[:, col] * xin[:, col].astype(F32)
        opened = gate[:, col].astype(F32)
        out[:, col] = (mixed * (opened / (1.0 + jnp.exp(-opened)))).astype(BF16)


def finish(steps, drive, partials, rates, entering, xin, gate, skip):
    rows = xin.shape[0]
    out = jax.ShapeDtypeStruct(xin.shape, BF16)
    scratch = [
        pltpu.VMEM((rows * 2 * NS, LANES), F32),
        pltpu.VMEM(steps.shape, F32),
    ]
    estimate = cost(9 * steps.size * NS, 14 * steps.size, steps.size * NS)
    return local(final_body, out, scratch, 0, 14, estimate)(
        steps, drive, *partials, rates, *entering, xin, gate, skip.reshape(1, -1)
    )


def exchange(x, groups):
    return lax.all_to_all(x, "ctx", 0, 0, axis_index_groups=groups, tiled=True)


def after(part, distance):
    count = lax.axis_size("ctx")
    return lax.ppermute(part, "ctx", [(i, i + distance) for i in range(count - distance)])


def shards(query, key, value, xin, gate_z, w_bc, dt_low, dt_proj, dt_bias, a_rate, skip):
    ctx, tp = lax.axis_size("ctx"), lax.axis_size("tp")
    side, planes = 8, ctx // 16
    line = 2 * side
    index = lax.axis_index("ctx")
    place = index.astype(jnp.int32).reshape(1)
    along_y = [[z * line + 2 * y + c for y in range(side)] for z in range(planes) for c in (0, 1)]
    partner = [(i, i ^ 1) for i in range(ctx)]
    next_row = [(i, i + line) for i in range(ctx - line)]

    own_kv = exchange(pack(key, value), along_y)
    partial = project(xin, w_bc)
    partials = [partial] + [
        lax.ppermute(partial, "tp", [(i, (i + d) % tp) for i in range(tp)])
        for d in range(1, tp)
    ]
    steps, drive = step_sizes(dt_low, dt_proj, dt_bias, xin)
    ends, rates = block_ends(steps, drive, partials, a_rate)
    queries = pack(query)
    own_kv, queries = lax.optimization_barrier((own_kv, queries))
    queries = exchange(queries, along_y)
    other_kv = lax.ppermute(own_kv, "ctx", partner)
    old_kv = lax.ppermute(own_kv[side // 2 :], "ctx", next_row)
    past_kv = lax.ppermute(old_kv, "ctx", partner)
    ends = join(rates, [after(ends, 2), after(ends, 1)])
    for stride in (2, 8):
        ends = join(rates, [after(ends, d * stride) for d in (3, 2, 1)] + [ends])
    entering = [after(ends, d * 32) for d in (3, 2, 1)] + [ends]
    attended = attend(place, queries, own_kv, other_kv, old_kv, past_kv)
    attended = exchange(attended, along_y)
    attended = unpack(attended)
    mixed = finish(
        steps, drive, partials, rates, entering, xin, gate_z, skip
    )
    return (attended, mixed)


def solution(mesh):
    in_specs = (
        P("ctx", "tp"),
        P("ctx", "tp"),
        P("ctx", "tp"),
        P("ctx", "tp"),
        P("ctx", "tp"),
        P("tp", None),
        P("ctx", None),
        P(None, "tp"),
        P("tp"),
        P(None, "tp"),
        P("tp"),
    )
    out_specs = (P("ctx", "tp"), P("ctx", "tp"))
    return jax.shard_map(shards, mesh=mesh, in_specs=in_specs, out_specs=out_specs, check_vma=False)
```

```python
import jax
import jax.numpy as jnp
from jax import lax
from jax.experimental import pallas as pl
from jax.experimental.pallas import tpu as pltpu
from jax.sharding import PartitionSpec as P


HD = 128
WINDOW = 2048
NS = 16
LANES = 128
TILES = 8
LOG2E = 1.4426950408889634
F32 = jnp.float32
BF16 = jnp.bfloat16
VMEM = pl.BlockSpec(memory_space=pltpu.VMEM)
SMEM = pl.BlockSpec(memory_space=pltpu.SMEM)


def cost(flops, moved, exps=0):
    return pl.CostEstimate(flops=flops, bytes_accessed=moved, transcendentals=exps)


def local(body, outs, scratch=(), scalars=0, arrays=1, estimate=None, limit=48 << 20):
    return pl.pallas_call(
        body,
        out_shape=outs,
        in_specs=[SMEM] * scalars + [VMEM] * arrays,
        out_specs=jax.tree.map(lambda _: VMEM, outs),
        scratch_shapes=list(scratch),
        cost_estimate=estimate,
        compiler_params=pltpu.CompilerParams(vmem_limit_bytes=limit),
    )


def parity_of(place):
    return place[0] & 1


def plane_of(place):
    return place[0] >> 4


def pack_body(*refs):
    *ins, out, sems = refs
    rows = ins[0].shape[0]
    copies = []
    for head in range(out.shape[0]):
        for k, part in enumerate(ins):
            source = part.at[:, pl.ds(head * HD, HD)]
            target = out.at[head, pl.ds(k * rows, rows), :]
            copies.append(pltpu.make_async_copy(source, target, sems.at[head, k]))
    for copy in copies:
        copy.start()
    for copy in copies:
        copy.wait()


def pack(*parts):
    rows, width = parts[0].shape
    heads = width // HD
    return pl.pallas_call(
        pack_body,
        out_shape=jax.ShapeDtypeStruct((heads, len(parts) * rows, HD), BF16),
        in_specs=[pl.BlockSpec(memory_space=pl.ANY)] * len(parts),
        out_specs=VMEM,
        scratch_shapes=[pltpu.SemaphoreType.DMA((heads, len(parts)))],
        name="pack",
        cost_estimate=cost(0, 4 * len(parts) * rows * width),
    )(*parts)


def unpack_body(blocks, out):
    for head in range(blocks.shape[0]):
        out[:, head * HD : (head + 1) * HD] = blocks[head]


def unpack(blocks):
    heads, rows, _ = blocks.shape
    out = jax.ShapeDtypeStruct((rows, heads * HD), BF16)
    return local(unpack_body, out, estimate=cost(0, 4 * rows * heads * HD))(blocks)


def weigh(q, edge_pair, full, out, i):
    rows = q.shape[0]
    scale = HD**-0.5 * LOG2E
    columns = lax.broadcasted_iota(jnp.int32, (rows, rows), 1)
    below = columns <= lax.broadcasted_iota(jnp.int32, (rows, rows), 0)

    def dots(keys):
        return lax.dot_general(q, keys, (((1,), (1,)), ((), ())), preferred_element_type=F32)

    def gather(weights, values, ones):
        side = jnp.concatenate([values, ones], axis=1)
        return jnp.dot(weights, side, preferred_element_type=F32)

    (k_near, v_near, one_near), (k_far, v_far, one_far) = edge_pair
    scores = [jnp.where(below, dots(k_near), dots(k_far))] + [dots(k) for k, _, _ in full]
    top = None
    for part in scores:
        for c in range(0, rows, LANES):
            piece = part[:, c : c + LANES]
            top = piece if top is None else jnp.maximum(top, piece)
    top = jnp.max(top, axis=1, keepdims=True) * scale
    weights = [jnp.exp2(part * scale - top) for part in scores]
    total = gather(jnp.where(below, weights[0], 0.0).astype(BF16), v_near, one_near)
    total += gather(jnp.where(below, 0.0, weights[0]).astype(BF16), v_far, one_far)
    for part, (_, values, ones) in zip(weights[1:], full):
        total += gather(part.astype(BF16), values, ones)
    out[i] = (total[:, 0:HD] / total[:, HD : 2 * HD]).astype(BF16)


def late_body(place, queries, own, other, out):
    half = out.shape[0]
    rows = queries.shape[1]
    parity = parity_of(place)
    ones = jnp.ones((rows, HD), BF16)

    def block(source, b):
        return source[b, 0:rows, :], source[b, rows : 2 * rows, :], ones

    for i in range(half):
        full = [block(own, i + 1 + j) for j in range(half - 1)]
        full += [block(other, i + parity + j) for j in range(half)]
        weigh(queries[half + i], (block(own, half + i), block(own, i)), full, out, i)


def early_body(place, queries, own, other, old, past, later, out, ko, kp):
    half = later.shape[0]
    rows = queries.shape[1]
    even = parity_of(place) == 0
    live = plane_of(place) > 0
    out[half:] = later[...]
    key0 = jnp.where(even, own[0, 0:1, :].astype(F32), other[0, 0:1, :].astype(F32))
    key0 = jnp.broadcast_to(key0, (rows, HD)).astype(BF16)
    ones = jnp.ones((rows, HD), BF16)
    shown = jnp.where(live, jnp.ones((rows, HD), F32), jnp.zeros((rows, HD), F32)).astype(BF16)
    for keys, source in ((ko, old), (kp, past)):

        @pl.when(live)
        def _():
            for b in range(half):
                keys[b] = source[b, 0:rows, :]

        @pl.when(jnp.logical_not(live))
        def _():
            for b in range(half):
                keys[b] = key0

    def new(source, b):
        return source[b, 0:rows, :], source[b, rows : 2 * rows, :], ones

    def before(keys, source, b):
        return keys[b], source[b, rows : 2 * rows, :], shown

    def mine(b):
        return before(ko, old, b) if b < half else new(own, b - half)

    def either(first, second):
        return tuple(
            jnp.where(even, a.astype(F32), b.astype(F32)).astype(BF16) for a, b in zip(first, second)
        )

    def theirs(b):
        if b + 1 < half:
            at = b + parity_of(place)
            return kp[at], past[at, rows : 2 * rows, :], shown
        if b >= half:
            at = b - half + parity_of(place)
            return other[at, 0:rows, :], other[at, rows : 2 * rows, :], ones
        return either(before(kp, past, b), new(other, 0))

    for i in range(half):
        full = [mine(i + 1 + j) for j in range(half - 1)] + [theirs(i + j) for j in range(half)]
        weigh(queries[i], (mine(half + i), mine(i)), full, out, i)


def attend_late(place, queries, own, other):
    blocks, rows, _ = queries.shape
    half = blocks // 2
    out = jax.ShapeDtypeStruct((half, rows, HD), BF16)
    estimate = cost(4 * half * rows * WINDOW * 2 * HD, 4 << 20, half * rows * WINDOW)
    return local(late_body, out, (), 1, 3, estimate)(place, queries, own, other)


def attend_early(place, queries, own, other, old, past, later):
    blocks, rows, _ = queries.shape
    half = blocks // 2
    scratch = [pltpu.VMEM((half, rows, HD), BF16)] * 2
    out = jax.ShapeDtypeStruct(queries.shape, BF16)
    estimate = cost(4 * half * rows * WINDOW * 2 * HD, 4 << 20, half * rows * WINDOW)
    return local(early_body, out, scratch, 1, 6, estimate)(
        place, queries, own, other, old, past, later
    )


def rows_of(step):
    return pl.ds(pl.multiple_of(step * TILES, TILES), TILES)


def project_body(xin, w_bc, out):
    out[...] = jnp.dot(xin[...], w_bc[...], preferred_element_type=F32).T


def project(xin, w_bc):
    out = jax.ShapeDtypeStruct((w_bc.shape[1], xin.shape[0]), F32)
    return local(project_body, out, arrays=2, estimate=cost(0, 2 * xin.size))(xin, w_bc)


def load_steps(low, proj, bias, xin, steps, drive):
    rows = low.shape[0]
    for c in range(TILES):
        col = slice(c * LANES, (c + 1) * LANES)
        raw = jnp.dot(low[...], proj[:, col], preferred_element_type=F32) + bias[:, col]
        size = jnp.maximum(raw, 0.0) + jnp.log1p(jnp.exp(-jnp.abs(raw)))
        steps[pl.ds(c, rows, stride=TILES), :] = size
        drive[pl.ds(c, rows, stride=TILES), :] = size * xin[:, col].astype(F32)


def spread(parts, count, wide):
    total = parts[0][0:count, :]
    for part in parts[1:]:
        total = total + part[0:count, :]
    total = total.T
    rows = total.shape[0]
    for n in range(count):
        column = jnp.broadcast_to(total[:, n : n + 1], (rows, LANES))
        wide[pl.ds(n, rows, stride=count), :] = column


def load_rates(a_rate, held):
    for c in range(TILES):
        held[pl.ds(c, NS, stride=TILES), :] = a_rate[:, c * LANES : (c + 1) * LANES] * -LOG2E
    return [held[n * TILES : (n + 1) * TILES, :] for n in range(NS)]


def ends_body(low, proj, bias, xin, p0, p1, p2, p3, a_rate, out, held, wide, steps, drive):
    rows = p0.shape[1]
    load_steps(low, proj, bias, xin, steps, drive)
    spread((p0, p1, p2, p3), NS, wide)
    rates = load_rates(a_rate, held)

    def step(t, carry):
        state, through = carry
        size, push = steps[rows_of(t), :], drive[rows_of(t), :]
        state = tuple(
            jnp.exp2(size * rates[n]) * state[n] + push * wide[pl.ds(t * NS + n, 1), :]
            for n in range(NS)
        )
        return state, through + size

    zero = jnp.zeros((TILES, LANES), F32)
    state, through = lax.fori_loop(0, rows, step, ((zero,) * NS, zero), unroll=4)
    for n in range(NS):
        out[n * TILES : (n + 1) * TILES, :] = state[n]
    out[NS * TILES :, :] = through


def block_ends(sources, partials, a_rate):
    rows, width = sources[3].shape
    out = jax.ShapeDtypeStruct(((NS + 1) * TILES, LANES), F32)
    rates = jax.ShapeDtypeStruct((NS * TILES, LANES), F32)
    scratch = [pltpu.VMEM((rows * NS, LANES), F32)] + [pltpu.VMEM((rows * TILES, LANES), F32)] * 2
    estimate = cost(6 * rows * width * NS, 4 * rows * width, rows * width * NS)
    return local(ends_body, (out, rates), scratch, 0, 9, estimate)(*sources, *partials, a_rate)


def fold(rates, parts):
    state = [parts[0][n * TILES : (n + 1) * TILES, :] for n in range(NS)]
    through = parts[0][NS * TILES :, :]
    for part in parts[1:]:
        size = part[NS * TILES :, :]
        for n in range(NS):
            row = slice(n * TILES, (n + 1) * TILES)
            state[n] = jnp.exp2(size * rates[row, :]) * state[n] + part[row, :]
        through = through + size
    return state, through


def join_body(rates, *refs):
    *parts, out = refs
    state, through = fold(rates, parts)
    for n in range(NS):
        out[n * TILES : (n + 1) * TILES, :] = state[n]
    out[NS * TILES :, :] = through


def join(rates, parts):
    out = jax.ShapeDtypeStruct(parts[0].shape, F32)
    estimate = cost(1 << 16, 1 << 18)
    return local(join_body, out, arrays=1 + len(parts), estimate=estimate)(rates, *parts)


def final_body(
    low, proj, bias, xin, p0, p1, p2, p3, held, e0, e1, gate, skip, out, wide, mix, steps, drive
):
    rows = p0.shape[1]
    load_steps(low, proj, bias, xin, steps, drive)
    spread((p0, p1, p2, p3), 2 * NS, wide)
    rates = [held[n * TILES : (n + 1) * TILES, :] for n in range(NS)]
    state, _ = fold(held, (e0, e1))

    def step(t, state):
        size, push = steps[rows_of(t), :], drive[rows_of(t), :]
        after = []
        result = None
        for n in range(NS):
            at = t * 2 * NS + n
            now = jnp.exp2(size * rates[n]) * state[n] + push * wide[pl.ds(at, 1), :]
            after.append(now)
            term = now * wide[pl.ds(at + NS, 1), :]
            result = term if result is None else result + term
        mix[rows_of(t), :] = result
        return tuple(after)

    lax.fori_loop(0, rows, step, tuple(state), unroll=4)
    for c in range(TILES):
        col = slice(c * LANES, (c + 1) * LANES)
        mixed = mix[pl.ds(c, rows, stride=TILES), :] + skip[:, col] * xin[:, col].astype(F32)
        opened = gate[:, col].astype(F32)
        out[:, col] = (mixed * (opened / (1.0 + jnp.exp(-opened)))).astype(BF16)


def finish(sources, partials, rates, entering, gate, skip):
    rows, width = gate.shape
    out = jax.ShapeDtypeStruct(gate.shape, BF16)
    tall = pltpu.VMEM((rows * TILES, LANES), F32)
    scratch = [pltpu.VMEM((rows * 2 * NS, LANES), F32), tall, tall, tall]
    estimate = cost(9 * rows * width * NS, 8 * rows * width, rows * width * NS)
    return local(final_body, out, scratch, 0, 13, estimate)(
        *sources, *partials, rates, *entering, gate, skip.reshape(1, -1)
    )


def exchange(x, groups):
    return lax.all_to_all(x, "ctx", 0, 0, axis_index_groups=groups, tiled=True)


def after(part, distance):
    count = lax.axis_size("ctx")
    return lax.ppermute(part, "ctx", [(i, i + distance) for i in range(count - distance)])


def shards(query, key, value, xin, gate_z, w_bc, dt_low, dt_proj, dt_bias, a_rate, skip):
    ctx, tp = lax.axis_size("ctx"), lax.axis_size("tp")
    side, planes = 8, ctx // 16
    line = 2 * side
    index = lax.axis_index("ctx")
    place = index.astype(jnp.int32).reshape(1)
    along_y = [[z * line + 2 * y + c for y in range(side)] for z in range(planes) for c in (0, 1)]
    partner = [(i, i ^ 1) for i in range(ctx)]
    next_row = [(i, i + line) for i in range(ctx - line)]

    own_kv = exchange(pack(key, value), along_y)
    partial = project(xin, w_bc)
    partials = [partial] + [
        lax.ppermute(partial, "tp", [(i, (i + d) % tp) for i in range(tp)])
        for d in range(1, tp)
    ]
    sources = (dt_low, dt_proj, dt_bias.reshape(1, -1), xin)
    ends, rates = block_ends(sources, partials, a_rate)
    queries = pack(query)
    own_kv, queries = lax.optimization_barrier((own_kv, queries))
    queries = exchange(queries, along_y)
    old_kv = lax.ppermute(own_kv[side // 2 :], "ctx", next_row)
    other_kv = lax.ppermute(own_kv, "ctx", partner)
    past_kv = lax.ppermute(old_kv, "ctx", partner)
    ends = join(rates, [after(ends, 2), after(ends, 1)])
    ends = join(rates, [after(ends, 6), after(ends, 4), after(ends, 2), ends])
    ends = join(rates, [after(ends, 8), ends])
    ends = join(rates, [after(ends, 48), after(ends, 32), after(ends, 16), ends])
    entering = [after(ends, 64), ends]
    later = attend_late(place, queries, own_kv, other_kv)
    attended = attend_early(place, queries, own_kv, other_kv, old_kv, past_kv, later)
    attended = exchange(attended, along_y)
    attended = unpack(attended)
    mixed = finish(sources, partials, rates, entering, gate_z, skip)
    return (attended, mixed)


def solution(mesh):
    in_specs = (
        P("ctx", "tp"),
        P("ctx", "tp"),
        P("ctx", "tp"),
        P("ctx", "tp"),
        P("ctx", "tp"),
        P("tp", None),
        P("ctx", None),
        P(None, "tp"),
        P("tp"),
        P(None, "tp"),
        P("tp"),
    )
    out_specs = (P("ctx", "tp"), P("ctx", "tp"))
    return jax.shard_map(shards, mesh=mesh, in_specs=in_specs, out_specs=out_specs, check_vma=False)
```

```python
import jax
import jax.numpy as jnp
from jax import lax
from jax.experimental import pallas as pl
from jax.experimental.pallas import tpu as pltpu
from jax.sharding import PartitionSpec as P


HD = 128
WINDOW = 2048
NS = 16
LANES = 128
TILES = 8
LOG2E = 1.4426950408889634
F32 = jnp.float32
BF16 = jnp.bfloat16
VMEM = pl.BlockSpec(memory_space=pltpu.VMEM)
SMEM = pl.BlockSpec(memory_space=pltpu.SMEM)


def cost(flops, moved, exps=0):
    return pl.CostEstimate(flops=flops, bytes_accessed=moved, transcendentals=exps)


def local(body, outs, scratch=(), scalars=0, arrays=1, estimate=None, limit=48 << 20):
    return pl.pallas_call(
        body,
        out_shape=outs,
        in_specs=[SMEM] * scalars + [VMEM] * arrays,
        out_specs=jax.tree.map(lambda _: VMEM, outs),
        scratch_shapes=list(scratch),
        cost_estimate=estimate,
        compiler_params=pltpu.CompilerParams(vmem_limit_bytes=limit),
    )


def parity_of(place):
    return place[0] & 1


def plane_of(place):
    return place[0] >> 4


def pack_body(*refs):
    *ins, out, sems = refs
    rows = ins[0].shape[0]
    copies = []
    for head in range(out.shape[0]):
        for k, part in enumerate(ins):
            source = part.at[:, pl.ds(head * HD, HD)]
            target = out.at[head, pl.ds(k * rows, rows), :]
            copies.append(pltpu.make_async_copy(source, target, sems.at[head, k]))
    for copy in copies:
        copy.start()
    for copy in copies:
        copy.wait()


def pack(*parts):
    rows, width = parts[0].shape
    heads = width // HD
    return pl.pallas_call(
        pack_body,
        out_shape=jax.ShapeDtypeStruct((heads, len(parts) * rows, HD), BF16),
        in_specs=[pl.BlockSpec(memory_space=pl.ANY)] * len(parts),
        out_specs=VMEM,
        scratch_shapes=[pltpu.SemaphoreType.DMA((heads, len(parts)))],
        name="pack",
        cost_estimate=cost(0, 4 * len(parts) * rows * width),
    )(*parts)


def unpack_body(blocks, out):
    for head in range(blocks.shape[0]):
        out[:, head * HD : (head + 1) * HD] = blocks[head]


def unpack(blocks):
    heads, rows, _ = blocks.shape
    out = jax.ShapeDtypeStruct((rows, heads * HD), BF16)
    return local(unpack_body, out, estimate=cost(0, 4 * rows * heads * HD))(blocks)


def weigh(q, edge_pair, full, out, i):
    rows = q.shape[0]
    scale = HD**-0.5 * LOG2E
    columns = lax.broadcasted_iota(jnp.int32, (rows, rows), 1)
    below = columns <= lax.broadcasted_iota(jnp.int32, (rows, rows), 0)

    def dots(keys):
        return lax.dot_general(q, keys, (((1,), (1,)), ((), ())), preferred_element_type=F32)

    def gather(weights, values, ones):
        side = jnp.concatenate([values, ones], axis=1)
        return jnp.dot(weights, side, preferred_element_type=F32)

    (k_near, v_near, one_near), (k_far, v_far, one_far) = edge_pair
    scores = [jnp.where(below, dots(k_near), dots(k_far))] + [dots(k) for k, _, _ in full]
    top = None
    for part in scores:
        for c in range(0, rows, LANES):
            piece = part[:, c : c + LANES]
            top = piece if top is None else jnp.maximum(top, piece)
    top = jnp.max(top, axis=1, keepdims=True) * scale
    weights = [jnp.exp2(part * scale - top) for part in scores]
    total = gather(jnp.where(below, weights[0], 0.0).astype(BF16), v_near, one_near)
    total += gather(jnp.where(below, 0.0, weights[0]).astype(BF16), v_far, one_far)
    for part, (_, values, ones) in zip(weights[1:], full):
        total += gather(part.astype(BF16), values, ones)
    out[i] = (total[:, 0:HD] / total[:, HD : 2 * HD]).astype(BF16)


def late_body(place, queries, own, other, out):
    half = out.shape[0]
    rows = queries.shape[1]
    parity = parity_of(place)
    ones = jnp.ones((rows, HD), BF16)

    def block(source, b):
        return source[b, 0:rows, :], source[b, rows : 2 * rows, :], ones

    for i in range(half):
        full = [block(own, i + 1 + j) for j in range(half - 1)]
        full += [block(other, i + parity + j) for j in range(half)]
        weigh(queries[half + i], (block(own, half + i), block(own, i)), full, out, i)


def early_body(place, queries, own, other, old, past, later, out, ko, kp):
    half = later.shape[0]
    rows = queries.shape[1]
    even = parity_of(place) == 0
    live = plane_of(place) > 0
    out[half:] = later[...]
    key0 = jnp.where(even, own[0, 0:1, :].astype(F32), other[0, 0:1, :].astype(F32))
    key0 = jnp.broadcast_to(key0, (rows, HD)).astype(BF16)
    ones = jnp.ones((rows, HD), BF16)
    shown = jnp.where(live, jnp.ones((rows, HD), F32), jnp.zeros((rows, HD), F32)).astype(BF16)
    for keys, source in ((ko, old), (kp, past)):

        @pl.when(live)
        def _():
            for b in range(half):
                keys[b] = source[b, 0:rows, :]

        @pl.when(jnp.logical_not(live))
        def _():
            for b in range(half):
                keys[b] = key0

    def new(source, b):
        return source[b, 0:rows, :], source[b, rows : 2 * rows, :], ones

    def before(keys, source, b):
        return keys[b], source[b, rows : 2 * rows, :], shown

    def mine(b):
        return before(ko, old, b) if b < half else new(own, b - half)

    def either(first, second):
        return tuple(
            jnp.where(even, a.astype(F32), b.astype(F32)).astype(BF16) for a, b in zip(first, second)
        )

    def theirs(b):
        if b + 1 < half:
            at = b + parity_of(place)
            return kp[at], past[at, rows : 2 * rows, :], shown
        if b >= half:
            at = b - half + parity_of(place)
            return other[at, 0:rows, :], other[at, rows : 2 * rows, :], ones
        return either(before(kp, past, b), new(other, 0))

    for i in range(half):
        full = [mine(i + 1 + j) for j in range(half - 1)] + [theirs(i + j) for j in range(half)]
        weigh(queries[i], (mine(half + i), mine(i)), full, out, i)


def attend_late(place, queries, own, other):
    blocks, rows, _ = queries.shape
    half = blocks // 2
    out = jax.ShapeDtypeStruct((half, rows, HD), BF16)
    estimate = cost(4 * half * rows * WINDOW * 2 * HD, 4 << 20, half * rows * WINDOW)
    return local(late_body, out, (), 1, 3, estimate)(place, queries, own, other)


def attend_early(place, queries, own, other, old, past, later):
    blocks, rows, _ = queries.shape
    half = blocks // 2
    scratch = [pltpu.VMEM((half, rows, HD), BF16)] * 2
    out = jax.ShapeDtypeStruct(queries.shape, BF16)
    estimate = cost(4 * half * rows * WINDOW * 2 * HD, 4 << 20, half * rows * WINDOW)
    return local(early_body, out, scratch, 1, 6, estimate)(
        place, queries, own, other, old, past, later
    )


def rows_of(step):
    return pl.ds(pl.multiple_of(step * TILES, TILES), TILES)


def project_body(xin, w_bc, out):
    out[...] = jnp.dot(xin[...], w_bc[...], preferred_element_type=F32).T


def project(xin, w_bc):
    out = jax.ShapeDtypeStruct((w_bc.shape[1], xin.shape[0]), F32)
    return local(project_body, out, arrays=2, estimate=cost(0, 2 * xin.size))(xin, w_bc)


def load_steps(low, proj, bias, xin, steps, drive):
    rows = low.shape[0]
    for c in range(TILES):
        col = slice(c * LANES, (c + 1) * LANES)
        raw = jnp.dot(low[...], proj[:, col], preferred_element_type=F32) + bias[:, col]
        size = jnp.maximum(raw, 0.0) + jnp.log1p(jnp.exp(-jnp.abs(raw)))
        steps[pl.ds(c, rows, stride=TILES), :] = size
        drive[pl.ds(c, rows, stride=TILES), :] = size * xin[:, col].astype(F32)


def spread(parts, count, wide):
    total = parts[0, 0:count, :]
    for k in range(1, parts.shape[0]):
        total = total + parts[k, 0:count, :]
    total = total.T
    rows = total.shape[0]
    for n in range(count):
        column = jnp.broadcast_to(total[:, n : n + 1], (rows, LANES))
        wide[pl.ds(n, rows, stride=count), :] = column


def load_rates(a_rate, held):
    for c in range(TILES):
        held[pl.ds(c, NS, stride=TILES), :] = a_rate[:, c * LANES : (c + 1) * LANES] * -LOG2E
    return [held[n * TILES : (n + 1) * TILES, :] for n in range(NS)]


def ends_body(low, proj, bias, xin, partials, a_rate, out, held, wide, steps, drive):
    rows = xin.shape[0]
    load_steps(low, proj, bias, xin, steps, drive)
    spread(partials, NS, wide)
    rates = load_rates(a_rate, held)

    def step(t, carry):
        state, through = carry
        size, push = steps[rows_of(t), :], drive[rows_of(t), :]
        state = tuple(
            jnp.exp2(size * rates[n]) * state[n] + push * wide[pl.ds(t * NS + n, 1), :]
            for n in range(NS)
        )
        return state, through + size

    zero = jnp.zeros((TILES, LANES), F32)
    state, through = lax.fori_loop(0, rows, step, ((zero,) * NS, zero), unroll=4)
    for n in range(NS):
        out[n * TILES : (n + 1) * TILES, :] = state[n]
    out[NS * TILES :, :] = through


def block_ends(sources, partials, a_rate):
    rows, width = sources[3].shape
    out = jax.ShapeDtypeStruct(((NS + 1) * TILES, LANES), F32)
    rates = jax.ShapeDtypeStruct((NS * TILES, LANES), F32)
    scratch = [pltpu.VMEM((rows * NS, LANES), F32)] + [pltpu.VMEM((rows * TILES, LANES), F32)] * 2
    estimate = cost(6 * rows * width * NS, 4 * rows * width, rows * width * NS)
    return local(ends_body, (out, rates), scratch, 0, 6, estimate)(*sources, partials, a_rate)


def fold(rates, state, through, part):
    size = part[NS * TILES :, :]
    out = []
    for n in range(NS):
        row = slice(n * TILES, (n + 1) * TILES)
        out.append(jnp.exp2(size * rates[row, :]) * state[n] + part[row, :])
    return out, through + size


def row_body(place, rates, blocks, before, whole):
    mine = place[0] & (blocks.shape[0] - 1)
    state = [jnp.zeros((TILES, LANES), F32)] * NS
    through = jnp.zeros((TILES, LANES), F32)
    held = state + [through]
    for k in range(blocks.shape[0]):
        here = mine == k
        held = [jnp.where(here, now, old) for now, old in zip(state + [through], held)]
        state, through = fold(rates, state, through, blocks[k])
    for n in range(NS + 1):
        row = slice(n * TILES, (n + 1) * TILES)
        before[row, :] = held[n]
        whole[row, :] = (state + [through])[n]


def join_row(place, rates, blocks):
    out = jax.ShapeDtypeStruct(blocks.shape[1:], F32)
    estimate = cost(1 << 20, 2 << 20)
    return local(row_body, (out, out), (), 1, 2, estimate)(place, rates, blocks)


def final_body(
    place, low, proj, bias, xin, partials, held, planes, before, gate, skip, out, wide, mix, steps, drive
):
    rows = xin.shape[0]
    load_steps(low, proj, bias, xin, steps, drive)
    spread(partials, 2 * NS, wide)
    rates = [held[n * TILES : (n + 1) * TILES, :] for n in range(NS)]
    state = [jnp.zeros((TILES, LANES), F32)] * NS
    through = jnp.zeros((TILES, LANES), F32)
    for z in range(planes.shape[0]):
        earlier = z < plane_of(place)
        later, _ = fold(held, state, through, planes[z])
        state = [jnp.where(earlier, new, old) for new, old in zip(later, state)]
    state, _ = fold(held, state, through, before)

    def step(t, state):
        size, push = steps[rows_of(t), :], drive[rows_of(t), :]
        after = []
        result = None
        for n in range(NS):
            at = t * 2 * NS + n
            now = jnp.exp2(size * rates[n]) * state[n] + push * wide[pl.ds(at, 1), :]
            after.append(now)
            term = now * wide[pl.ds(at + NS, 1), :]
            result = term if result is None else result + term
        mix[rows_of(t), :] = result
        return tuple(after)

    lax.fori_loop(0, rows, step, tuple(state), unroll=4)
    for c in range(TILES):
        col = slice(c * LANES, (c + 1) * LANES)
        mixed = mix[pl.ds(c, rows, stride=TILES), :] + skip[:, col] * xin[:, col].astype(F32)
        opened = gate[:, col].astype(F32)
        out[:, col] = (mixed * (opened / (1.0 + jnp.exp(-opened)))).astype(BF16)


def finish(place, sources, partials, rates, planes, before, gate, skip):
    rows, width = gate.shape
    out = jax.ShapeDtypeStruct(gate.shape, BF16)
    tall = pltpu.VMEM((rows * TILES, LANES), F32)
    scratch = [pltpu.VMEM((rows * 2 * NS, LANES), F32), tall, tall, tall]
    estimate = cost(9 * rows * width * NS, 8 * rows * width, rows * width * NS)
    return local(final_body, out, scratch, 1, 10, estimate)(
        place, *sources, partials, rates, planes, before, gate, skip.reshape(1, -1)
    )


def exchange(x, groups):
    return lax.all_to_all(x, "ctx", 0, 0, axis_index_groups=groups, tiled=True)


def shards(query, key, value, xin, gate_z, w_bc, dt_low, dt_proj, dt_bias, a_rate, skip):
    ctx = lax.axis_size("ctx")
    side, planes = 8, ctx // 16
    line = 2 * side
    index = lax.axis_index("ctx")
    place = index.astype(jnp.int32).reshape(1)
    along_y = [[z * line + 2 * y + c for y in range(side)] for z in range(planes) for c in (0, 1)]
    along_z = [[z * line + k for z in range(planes)] for k in range(line)]
    along_row = [[z * line + k for k in range(line)] for z in range(planes)]
    partner = [(i, i ^ 1) for i in range(ctx)]
    next_row = [(i, i + line) for i in range(ctx - line)]

    own_kv = exchange(pack(key, value), along_y)
    partial = project(xin, w_bc)
    partials = lax.all_gather(partial, "tp")
    sources = (dt_low, dt_proj, dt_bias.reshape(1, -1), xin)
    ends, rates = block_ends(sources, partials, a_rate)
    queries = pack(query)
    own_kv, queries = lax.optimization_barrier((own_kv, queries))
    queries = exchange(queries, along_y)
    old_kv = lax.ppermute(own_kv[side // 2 :], "ctx", next_row)
    other_kv = lax.ppermute(own_kv, "ctx", partner)
    past_kv = lax.ppermute(old_kv, "ctx", partner)
    blocks = lax.all_gather(ends, "ctx", axis_index_groups=along_row)
    before, whole = join_row(place, rates, blocks)
    wholes = lax.all_gather(whole, "ctx", axis_index_groups=along_z)
    later = attend_late(place, queries, own_kv, other_kv)
    attended = attend_early(place, queries, own_kv, other_kv, old_kv, past_kv, later)
    attended = exchange(attended, along_y)
    attended = unpack(attended)
    mixed = finish(place, sources, partials, rates, wholes, before, gate_z, skip)
    return (attended, mixed)


def solution(mesh):
    in_specs = (
        P("ctx", "tp"),
        P("ctx", "tp"),
        P("ctx", "tp"),
        P("ctx", "tp"),
        P("ctx", "tp"),
        P("tp", None),
        P("ctx", None),
        P(None, "tp"),
        P("tp"),
        P(None, "tp"),
        P("tp"),
    )
    out_specs = (P("ctx", "tp"), P("ctx", "tp"))
    return jax.shard_map(shards, mesh=mesh, in_specs=in_specs, out_specs=out_specs, check_vma=False)
```

```python
import functools

import jax
import jax.numpy as jnp
from jax import lax
from jax.experimental import pallas as pl
from jax.experimental.pallas import tpu as pltpu
from jax.sharding import PartitionSpec as P


HD = 128
WINDOW = 2048
NS = 16
LANES = 128
TILES = 8
LOG2E = 1.4426950408889634
F32 = jnp.float32
BF16 = jnp.bfloat16
VMEM = pl.BlockSpec(memory_space=pltpu.VMEM)
SMEM = pl.BlockSpec(memory_space=pltpu.SMEM)


def cost(flops, moved, exps=0):
    return pl.CostEstimate(flops=flops, bytes_accessed=moved, transcendentals=exps)


def local(body, outs, scratch=(), scalars=0, arrays=1, estimate=None, limit=48 << 20):
    return pl.pallas_call(
        body,
        out_shape=outs,
        in_specs=[SMEM] * scalars + [VMEM] * arrays,
        out_specs=jax.tree.map(lambda _: VMEM, outs),
        scratch_shapes=list(scratch),
        cost_estimate=estimate,
        compiler_params=pltpu.CompilerParams(vmem_limit_bytes=limit),
    )


def parity_of(place):
    return place[0] & 1


def plane_of(place):
    return place[0] >> 4


def pack_body(*refs):
    *ins, out, sems = refs
    rows = ins[0].shape[0]
    copies = []
    for head in range(out.shape[0]):
        for k, part in enumerate(ins):
            source = part.at[:, pl.ds(head * HD, HD)]
            target = out.at[head, pl.ds(k * rows, rows), :]
            copies.append(pltpu.make_async_copy(source, target, sems.at[head, k]))
    for copy in copies:
        copy.start()
    for copy in copies:
        copy.wait()


def pack(*parts):
    rows, width = parts[0].shape
    heads = width // HD
    return pl.pallas_call(
        pack_body,
        out_shape=jax.ShapeDtypeStruct((heads, len(parts) * rows, HD), BF16),
        in_specs=[pl.BlockSpec(memory_space=pl.ANY)] * len(parts),
        out_specs=VMEM,
        scratch_shapes=[pltpu.SemaphoreType.DMA((heads, len(parts)))],
        name="pack",
        cost_estimate=cost(0, 4 * len(parts) * rows * width),
    )(*parts)


def unpack_body(blocks, out):
    for head in range(blocks.shape[0]):
        out[:, head * HD : (head + 1) * HD] = blocks[head]


def unpack(blocks):
    heads, rows, _ = blocks.shape
    out = jax.ShapeDtypeStruct((rows, heads * HD), BF16)
    return local(unpack_body, out, estimate=cost(0, 4 * rows * heads * HD))(blocks)


def weigh(q, edge_pair, full, out, i):
    rows = q.shape[0]
    scale = HD**-0.5 * LOG2E
    columns = lax.broadcasted_iota(jnp.int32, (rows, rows), 1)
    below = columns <= lax.broadcasted_iota(jnp.int32, (rows, rows), 0)

    def dots(keys):
        return lax.dot_general(q, keys, (((1,), (1,)), ((), ())), preferred_element_type=F32)

    def gather(weights, values, ones):
        side = jnp.concatenate([values, ones], axis=1)
        return jnp.dot(weights, side, preferred_element_type=F32)

    (k_near, v_near, one_near), (k_far, v_far, one_far) = edge_pair
    scores = [jnp.where(below, dots(k_near), dots(k_far))] + [dots(k) for k, _, _ in full]
    top = None
    for part in scores:
        for c in range(0, rows, LANES):
            piece = part[:, c : c + LANES]
            top = piece if top is None else jnp.maximum(top, piece)
    top = jnp.max(top, axis=1, keepdims=True) * scale
    weights = [jnp.exp2(part * scale - top) for part in scores]
    total = gather(jnp.where(below, weights[0], 0.0).astype(BF16), v_near, one_near)
    total += gather(jnp.where(below, 0.0, weights[0]).astype(BF16), v_far, one_far)
    for part, (_, values, ones) in zip(weights[1:], full):
        total += gather(part.astype(BF16), values, ones)
    out[i] = (total[:, 0:HD] / total[:, HD : 2 * HD]).astype(BF16)


def late_body(place, own, other, out):
    half = out.shape[0]
    rows = out.shape[1]
    parity = parity_of(place)
    ones = jnp.ones((rows, HD), BF16)

    def block(source, b):
        return source[b, 0:rows, :], source[b, rows : 2 * rows, :], ones

    for i in range(half):
        full = [block(own, i + 1 + j) for j in range(half - 1)]
        full += [block(other, i + parity + j) for j in range(half)]
        weigh(own[half + i, 2 * rows :, :], (block(own, half + i), block(own, i)), full, out, i)


def early_body(place, own, other, old, past, later, out, ko, kp):
    half, rows, _ = later.shape
    even = parity_of(place) == 0
    live = plane_of(place) > 0
    out[half:] = later[...]
    key0 = jnp.where(even, own[0, 0:1, :].astype(F32), other[0, 0:1, :].astype(F32))
    key0 = jnp.broadcast_to(key0, (rows, HD)).astype(BF16)
    ones = jnp.ones((rows, HD), BF16)
    shown = jnp.where(live, jnp.ones((rows, HD), F32), jnp.zeros((rows, HD), F32)).astype(BF16)
    for keys, source in ((ko, old), (kp, past)):

        @pl.when(live)
        def _():
            for b in range(half):
                keys[b] = source[b, 0:rows, :]

        @pl.when(jnp.logical_not(live))
        def _():
            for b in range(half):
                keys[b] = key0

    def new(source, b):
        return source[b, 0:rows, :], source[b, rows : 2 * rows, :], ones

    def before(keys, source, b):
        return keys[b], source[b, rows : 2 * rows, :], shown

    def mine(b):
        return before(ko, old, b) if b < half else new(own, b - half)

    def either(first, second):
        return tuple(
            jnp.where(even, a.astype(F32), b.astype(F32)).astype(BF16) for a, b in zip(first, second)
        )

    def theirs(b):
        if b + 1 < half:
            at = b + parity_of(place)
            return kp[at], past[at, rows : 2 * rows, :], shown
        if b >= half:
            at = b - half + parity_of(place)
            return other[at, 0:rows, :], other[at, rows : 2 * rows, :], ones
        return either(before(kp, past, b), new(other, 0))

    for i in range(half):
        full = [mine(i + 1 + j) for j in range(half - 1)] + [theirs(i + j) for j in range(half)]
        weigh(own[i, 2 * rows :, :], (mine(half + i), mine(i)), full, out, i)


def attend_late(place, own, other):
    half, rows = own.shape[0] // 2, own.shape[1] // 3
    out = jax.ShapeDtypeStruct((half, rows, HD), BF16)
    estimate = cost(4 * half * rows * WINDOW * 2 * HD, 4 << 20, half * rows * WINDOW)
    return local(late_body, out, (), 1, 2, estimate)(place, own, other)


def attend_early(place, own, other, old, past, later):
    half, rows, _ = later.shape
    scratch = [pltpu.VMEM((half, rows, HD), BF16)] * 2
    out = jax.ShapeDtypeStruct((2 * half, rows, HD), BF16)
    estimate = cost(4 * half * rows * WINDOW * 2 * HD, 4 << 20, half * rows * WINDOW)
    return local(early_body, out, scratch, 1, 5, estimate)(place, own, other, old, past, later)


def rows_of(step):
    return pl.ds(pl.multiple_of(step * TILES, TILES), TILES)


def project_body(xin, w_bc, out):
    out[...] = jnp.dot(xin[...], w_bc[...], preferred_element_type=F32).T


def project(xin, w_bc):
    out = jax.ShapeDtypeStruct((w_bc.shape[1], xin.shape[0]), F32)
    return local(project_body, out, arrays=2, estimate=cost(0, 2 * xin.size))(xin, w_bc)


def load_steps(low, proj, bias, xin, steps, drive):
    rows = low.shape[0]
    for c in range(TILES):
        col = slice(c * LANES, (c + 1) * LANES)
        raw = jnp.dot(low[...], proj[:, col], preferred_element_type=F32) + bias[:, col]
        size = jnp.maximum(raw, 0.0) + jnp.log1p(jnp.exp(-jnp.abs(raw)))
        steps[pl.ds(c, rows, stride=TILES), :] = size
        drive[pl.ds(c, rows, stride=TILES), :] = size * xin[:, col].astype(F32)


def spread(parts, count, wide):
    total = parts[0][0:count, :]
    for part in parts[1:]:
        total = total + part[0:count, :]
    total = total.T
    rows = total.shape[0]
    for n in range(count):
        column = jnp.broadcast_to(total[:, n : n + 1], (rows, LANES))
        wide[pl.ds(n, rows, stride=count), :] = column


def load_rates(a_rate, held):
    for c in range(TILES):
        held[pl.ds(c, NS, stride=TILES), :] = a_rate[:, c * LANES : (c + 1) * LANES] * -LOG2E
    return [held[n * TILES : (n + 1) * TILES, :] for n in range(NS)]


def ends_body(low, proj, bias, xin, p0, p1, p2, p3, a_rate, out, held, wide, steps, drive):
    rows = p0.shape[1]
    load_steps(low, proj, bias, xin, steps, drive)
    spread((p0, p1, p2, p3), NS, wide)
    rates = load_rates(a_rate, held)

    def step(t, carry):
        state, through = carry
        size, push = steps[rows_of(t), :], drive[rows_of(t), :]
        state = tuple(
            jnp.exp2(size * rates[n]) * state[n] + push * wide[pl.ds(t * NS + n, 1), :]
            for n in range(NS)
        )
        return state, through + size

    zero = jnp.zeros((TILES, LANES), F32)
    state, through = lax.fori_loop(0, rows, step, ((zero,) * NS, zero), unroll=4)
    for n in range(NS):
        out[n * TILES : (n + 1) * TILES, :] = state[n]
    out[NS * TILES :, :] = through


def block_ends(sources, partials, a_rate):
    rows, width = sources[3].shape
    out = jax.ShapeDtypeStruct(((NS + 1) * TILES, LANES), F32)
    rates = jax.ShapeDtypeStruct((NS * TILES, LANES), F32)
    scratch = [pltpu.VMEM((rows * NS, LANES), F32)] + [pltpu.VMEM((rows * TILES, LANES), F32)] * 2
    estimate = cost(6 * rows * width * NS, 4 * rows * width, rows * width * NS)
    return local(ends_body, (out, rates), scratch, 0, 9, estimate)(*sources, *partials, a_rate)


def fold(rates, state, through, part):
    size = part[NS * TILES :, :]
    out = []
    for n in range(NS):
        row = slice(n * TILES, (n + 1) * TILES)
        out.append(jnp.exp2(size * rates[row, :]) * state[n] + part[row, :])
    return out, through + size


def nothing():
    zero = jnp.zeros((TILES, LANES), F32)
    return [zero] * NS, zero


def keep(out, state, through):
    for n in range(NS):
        out[n * TILES : (n + 1) * TILES, :] = state[n]
    out[NS * TILES :, :] = through


def join_body(shift, bits, *refs):
    place, rates, *rest = refs
    maps, rest = rest[: 1 << bits], rest[1 << bits :]
    before = rest[0] if len(rest) == 3 else None
    whole_out, before_out = rest[-2:]
    spot = (place[0] >> shift) & ((1 << bits) - 1)
    state, through = nothing()
    held_state, held_through = nothing()
    for k in range(1 << bits):
        here = spot == k
        held_state = [jnp.where(here, now, old) for now, old in zip(state, held_state)]
        held_through = jnp.where(here, through, held_through)
        part = maps[0][...]
        for distance in range(1, 1 << bits):
            part = jnp.where((spot ^ k) == distance, maps[distance][...], part)
        state, through = fold(rates, state, through, part)
    if len(whole_out.shape) == 3:
        for z in range(whole_out.shape[0]):
            keep(whole_out.at[z], state, through)
    else:
        keep(whole_out, state, through)
    if before is not None:
        held_state, held_through = fold(rates, held_state, held_through, before)
    keep(before_out, held_state, held_through)


def join(place, rates, maps, before, shift, copies):
    bits = len(maps).bit_length() - 1
    one = jax.ShapeDtypeStruct(maps[0].shape, F32)
    whole = jax.ShapeDtypeStruct((copies, *maps[0].shape), F32) if copies else one
    given = [rates, *maps] + ([] if before is None else [before])
    body = functools.partial(join_body, shift, bits)
    estimate = cost(1 << 18, 1 << 19)
    return local(body, (whole, one), (), 1, len(given), estimate)(place, *given)


def final_body(
    place, low, proj, bias, xin, p0, p1, p2, p3, held, planes, before, gate, skip,
    out, wide, mix, steps, drive,
):
    rows = p0.shape[1]
    load_steps(low, proj, bias, xin, steps, drive)
    spread((p0, p1, p2, p3), 2 * NS, wide)
    rates = [held[n * TILES : (n + 1) * TILES, :] for n in range(NS)]
    state, through = nothing()
    for z in range(planes.shape[0]):
        earlier = z < plane_of(place)
        later, _ = fold(held, state, through, planes[z])
        state = [jnp.where(earlier, new, old) for new, old in zip(later, state)]
    state, _ = fold(held, state, through, before)

    def step(t, state):
        size, push = steps[rows_of(t), :], drive[rows_of(t), :]
        after = []
        result = None
        for n in range(NS):
            at = t * 2 * NS + n
            now = jnp.exp2(size * rates[n]) * state[n] + push * wide[pl.ds(at, 1), :]
            after.append(now)
            term = now * wide[pl.ds(at + NS, 1), :]
            result = term if result is None else result + term
        mix[rows_of(t), :] = result
        return tuple(after)

    lax.fori_loop(0, rows, step, tuple(state), unroll=4)
    for c in range(TILES):
        col = slice(c * LANES, (c + 1) * LANES)
        mixed = mix[pl.ds(c, rows, stride=TILES), :] + skip[:, col] * xin[:, col].astype(F32)
        opened = gate[:, col].astype(F32)
        out[:, col] = (mixed * (opened / (1.0 + jnp.exp(-opened)))).astype(BF16)


def finish(place, sources, partials, rates, planes, before, gate, skip):
    rows, width = gate.shape
    out = jax.ShapeDtypeStruct(gate.shape, BF16)
    tall = pltpu.VMEM((rows * TILES, LANES), F32)
    scratch = [pltpu.VMEM((rows * 2 * NS, LANES), F32), tall, tall, tall]
    estimate = cost(9 * rows * width * NS, 8 * rows * width, rows * width * NS)
    return local(final_body, out, scratch, 1, 13, estimate)(
        place, *sources, *partials, rates, planes, before, gate, skip.reshape(1, -1)
    )


def exchange(x, groups):
    return lax.all_to_all(x, "ctx", 0, 0, axis_index_groups=groups, tiled=True)


def across(part, distance):
    count = lax.axis_size("ctx")
    return lax.ppermute(part, "ctx", [(i, i ^ distance) for i in range(count)])


def shards(query, key, value, xin, gate_z, w_bc, dt_low, dt_proj, dt_bias, a_rate, skip):
    ctx, tp = lax.axis_size("ctx"), lax.axis_size("tp")
    side, planes = 8, ctx // 16
    line = 2 * side
    index = lax.axis_index("ctx")
    place = index.astype(jnp.int32).reshape(1)
    along_y = [[z * line + 2 * y + c for y in range(side)] for z in range(planes) for c in (0, 1)]
    partner = [(i, i ^ 1) for i in range(ctx)]
    next_row = [(i, i + line) for i in range(ctx - line)]

    along_z = [[z * line + k for z in range(planes)] for k in range(line)]
    own = exchange(pack(key, value, query), along_y)
    partial = project(xin, w_bc)
    partials = [partial] + [
        lax.ppermute(partial, "tp", [(i, (i + d) % tp) for i in range(tp)])
        for d in range(1, tp)
    ]
    sources = (dt_low, dt_proj, dt_bias.reshape(1, -1), xin)
    ends, rates = block_ends(sources, partials, a_rate)
    whole, before = join(place, rates, [ends, across(ends, 1)], None, 0, 0)
    maps = [whole] + [across(whole, 2 * d) for d in (1, 2, 3)]
    whole, before = join(place, rates, maps, before, 1, 0)
    whole, before = join(place, rates, [whole, across(whole, 8)], before, 3, planes)
    old_kv = lax.ppermute(own[side // 2 :, : 2 * key.shape[0]], "ctx", next_row)
    wholes = exchange(whole, along_z)
    other = lax.ppermute(own, "ctx", partner)
    past_kv = lax.ppermute(old_kv, "ctx", partner)
    later = attend_late(place, own, other)
    attended = attend_early(place, own, other, old_kv, past_kv, later)
    attended = exchange(attended, along_y)
    attended = unpack(attended)
    mixed = finish(place, sources, partials, rates, wholes, before, gate_z, skip)
    return (attended, mixed)


def solution(mesh):
    in_specs = (
        P("ctx", "tp"),
        P("ctx", "tp"),
        P("ctx", "tp"),
        P("ctx", "tp"),
        P("ctx", "tp"),
        P("tp", None),
        P("ctx", None),
        P(None, "tp"),
        P("tp"),
        P(None, "tp"),
        P("tp"),
    )
    out_specs = (P("ctx", "tp"), P("ctx", "tp"))
    return jax.shard_map(shards, mesh=mesh, in_specs=in_specs, out_specs=out_specs, check_vma=False)
```

```python
import functools

import jax
import jax.numpy as jnp
from jax import lax
from jax.experimental import pallas as pl
from jax.experimental.pallas import tpu as pltpu
from jax.sharding import PartitionSpec as P


HD = 128
WINDOW = 2048
NS = 16
HALF = NS // 2
LANES = 128
TILES = 8
LOG2E = 1.4426950408889634
F32 = jnp.float32
BF16 = jnp.bfloat16
VMEM = pl.BlockSpec(memory_space=pltpu.VMEM)
SMEM = pl.BlockSpec(memory_space=pltpu.SMEM)


def cost(flops, moved, exps=0):
    return pl.CostEstimate(flops=flops, bytes_accessed=moved, transcendentals=exps)


def local(body, outs, scratch=(), scalars=0, arrays=1, estimate=None, limit=20 << 20):
    return pl.pallas_call(
        body,
        out_shape=outs,
        in_specs=[SMEM] * scalars + [VMEM] * arrays,
        out_specs=jax.tree.map(lambda _: VMEM, outs),
        scratch_shapes=list(scratch),
        cost_estimate=estimate,
        compiler_params=pltpu.CompilerParams(vmem_limit_bytes=limit),
    )


def parity_of(place):
    return place[0] & 1


def plane_of(place):
    return place[0] >> 4


def pack_body(*refs):
    *ins, out, sems = refs
    rows = ins[0].shape[0]
    copies = []
    for head in range(out.shape[0]):
        for k, part in enumerate(ins):
            source = part.at[:, pl.ds(head * HD, HD)]
            target = out.at[head, pl.ds(k * rows, rows), :]
            copies.append(pltpu.make_async_copy(source, target, sems.at[head, k]))
    for copy in copies:
        copy.start()
    for copy in copies:
        copy.wait()


def pack(*parts):
    rows, width = parts[0].shape
    heads = width // HD
    return pl.pallas_call(
        pack_body,
        out_shape=jax.ShapeDtypeStruct((heads, len(parts) * rows, HD), BF16),
        in_specs=[pl.BlockSpec(memory_space=pl.ANY)] * len(parts),
        out_specs=VMEM,
        scratch_shapes=[pltpu.SemaphoreType.DMA((heads, len(parts)))],
        name="pack",
        cost_estimate=cost(0, 4 * len(parts) * rows * width),
    )(*parts)


def unpack_body(blocks, out):
    for head in range(blocks.shape[0]):
        out[:, head * HD : (head + 1) * HD] = blocks[head]


def unpack(blocks):
    heads, rows, _ = blocks.shape
    out = jax.ShapeDtypeStruct((rows, heads * HD), BF16)
    return local(unpack_body, out, estimate=cost(0, 4 * rows * heads * HD))(blocks)


def weigh(q, edge_pair, full, out, i):
    rows = q.shape[0]
    scale = HD**-0.5 * LOG2E
    columns = lax.broadcasted_iota(jnp.int32, (rows, rows), 1)
    below = columns <= lax.broadcasted_iota(jnp.int32, (rows, rows), 0)

    def dots(keys):
        return lax.dot_general(q, keys, (((1,), (1,)), ((), ())), preferred_element_type=F32)

    def gather(weights, values, ones):
        side = jnp.concatenate([values, ones], axis=1)
        return jnp.dot(weights, side, preferred_element_type=F32)

    (k_near, v_near, one_near), (k_far, v_far, one_far) = edge_pair
    scores = [jnp.where(below, dots(k_near), dots(k_far))] + [dots(k) for k, _, _ in full]
    top = None
    for part in scores:
        for c in range(0, rows, LANES):
            piece = part[:, c : c + LANES]
            top = piece if top is None else jnp.maximum(top, piece)
    top = jnp.max(top, axis=1, keepdims=True) * scale
    weights = [jnp.exp2(part * scale - top) for part in scores]
    total = gather(jnp.where(below, weights[0], 0.0).astype(BF16), v_near, one_near)
    total += gather(jnp.where(below, 0.0, weights[0]).astype(BF16), v_far, one_far)
    for part, (_, values, ones) in zip(weights[1:], full):
        total += gather(part.astype(BF16), values, ones)
    out[i] = (total[:, 0:HD] / total[:, HD : 2 * HD]).astype(BF16)


def late_body(place, queries, own, other, out):
    half = out.shape[0]
    rows = out.shape[1]
    parity = parity_of(place)
    ones = jnp.ones((rows, HD), BF16)

    def block(source, b):
        return source[b, 0:rows, :], source[b, rows : 2 * rows, :], ones

    for i in range(half):
        full = [block(own, i + 1 + j) for j in range(half - 1)]
        full += [block(other, i + parity + j) for j in range(half)]
        weigh(queries[half + i], (block(own, half + i), block(own, i)), full, out, i)


def early_body(place, queries, own, other, old, past, later, out, ko, kp):
    half, rows, _ = later.shape
    even = parity_of(place) == 0
    live = plane_of(place) > 0
    out[half:] = later[...]
    key0 = jnp.where(even, own[0, 0:1, :].astype(F32), other[0, 0:1, :].astype(F32))
    key0 = jnp.broadcast_to(key0, (rows, HD)).astype(BF16)
    ones = jnp.ones((rows, HD), BF16)
    shown = jnp.where(live, jnp.ones((rows, HD), F32), jnp.zeros((rows, HD), F32)).astype(BF16)
    for keys, source in ((ko, old), (kp, past)):

        @pl.when(live)
        def _():
            for b in range(half):
                keys[b] = source[b, 0:rows, :]

        @pl.when(jnp.logical_not(live))
        def _():
            for b in range(half):
                keys[b] = key0

    def new(source, b):
        return source[b, 0:rows, :], source[b, rows : 2 * rows, :], ones

    def before(keys, source, b):
        return keys[b], source[b, rows : 2 * rows, :], shown

    def mine(b):
        return before(ko, old, b) if b < half else new(own, b - half)

    def either(first, second):
        return tuple(
            jnp.where(even, a.astype(F32), b.astype(F32)).astype(BF16) for a, b in zip(first, second)
        )

    def theirs(b):
        if b + 1 < half:
            at = b + parity_of(place)
            return kp[at], past[at, rows : 2 * rows, :], shown
        if b >= half:
            at = b - half + parity_of(place)
            return other[at, 0:rows, :], other[at, rows : 2 * rows, :], ones
        return either(before(kp, past, b), new(other, 0))

    for i in range(half):
        full = [mine(i + 1 + j) for j in range(half - 1)] + [theirs(i + j) for j in range(half)]
        weigh(queries[i], (mine(half + i), mine(i)), full, out, i)


def attend_late(place, queries, own, other):
    half, rows = queries.shape[0] // 2, queries.shape[1]
    out = jax.ShapeDtypeStruct((half, rows, HD), BF16)
    estimate = cost(4 * half * rows * WINDOW * 2 * HD, 4 << 20, half * rows * WINDOW)
    return local(late_body, out, (), 1, 3, estimate)(place, queries, own, other)


def attend_early(place, queries, own, other, old, past, later):
    half, rows, _ = later.shape
    scratch = [pltpu.VMEM((half, rows, HD), BF16)] * 2
    out = jax.ShapeDtypeStruct((2 * half, rows, HD), BF16)
    estimate = cost(4 * half * rows * WINDOW * 2 * HD, 4 << 20, half * rows * WINDOW)
    return local(early_body, out, scratch, 1, 6, estimate)(
        place, queries, own, other, old, past, later
    )


def rows_of(step):
    return pl.ds(pl.multiple_of(step * TILES, TILES), TILES)


def project_body(xin, w_bc, out):
    out[...] = jnp.dot(xin[...], w_bc[...], preferred_element_type=F32).T


def project(xin, w_bc):
    out = jax.ShapeDtypeStruct((w_bc.shape[1], xin.shape[0]), F32)
    return local(project_body, out, arrays=2, estimate=cost(0, 2 * xin.size))(xin, w_bc)


def load_steps(low, proj, bias, xin, steps, drive):
    rows = low.shape[0]
    for c in range(TILES):
        col = slice(c * LANES, (c + 1) * LANES)
        raw = jnp.dot(low[...], proj[:, col], preferred_element_type=F32) + bias[:, col]
        size = jnp.maximum(raw, 0.0) + jnp.log1p(jnp.exp(-jnp.abs(raw)))
        steps[pl.ds(c, rows, stride=TILES), :] = size
        drive[pl.ds(c, rows, stride=TILES), :] = size * xin[:, col].astype(F32)


def spread(parts, count, wide):
    total = parts[0][0:count, :]
    for part in parts[1:]:
        total = total + part[0:count, :]
    total = total.T
    rows = total.shape[0]
    for n in range(count):
        column = jnp.broadcast_to(total[:, n : n + 1], (rows, LANES))
        wide[pl.ds(n, rows, stride=count), :] = column


def load_rates(a_rate, held):
    for c in range(TILES):
        held[pl.ds(c, NS, stride=TILES), :] = a_rate[:, c * LANES : (c + 1) * LANES] * -LOG2E
    return [held[n * TILES : (n + 1) * TILES, :] for n in range(NS)]


def ends_body(low, proj, bias, xin, p0, p1, p2, p3, a_rate, out, held, wide, steps, drive):
    rows = p0.shape[1]
    load_steps(low, proj, bias, xin, steps, drive)
    spread((p0, p1, p2, p3), NS, wide)
    rates = load_rates(a_rate, held)

    def step(t, carry):
        state, through = carry
        size, push = steps[rows_of(t), :], drive[rows_of(t), :]
        state = tuple(
            jnp.exp2(size * rates[n]) * state[n] + push * wide[pl.ds(t * NS + n, 1), :]
            for n in range(NS)
        )
        return state, through + size

    zero = jnp.zeros((TILES, LANES), F32)
    state, through = lax.fori_loop(0, rows, step, ((zero,) * NS, zero), unroll=4)
    for n in range(NS):
        out[n * TILES : (n + 1) * TILES, :] = state[n]
    out[NS * TILES :, :] = through


def block_ends(sources, partials, a_rate):
    rows, width = sources[3].shape
    out = jax.ShapeDtypeStruct(((NS + 1) * TILES, LANES), F32)
    rates = jax.ShapeDtypeStruct((NS * TILES, LANES), F32)
    scratch = [pltpu.VMEM((rows * NS, LANES), F32)] + [pltpu.VMEM((rows * TILES, LANES), F32)] * 2
    estimate = cost(6 * rows * width * NS, 4 * rows * width, rows * width * NS)
    return local(ends_body, (out, rates), scratch, 0, 9, estimate)(*sources, *partials, a_rate)


def fold(rates, state, through, part):
    size = part[NS * TILES :, :]
    out = []
    for n in range(NS):
        row = slice(n * TILES, (n + 1) * TILES)
        out.append(jnp.exp2(size * rates[row, :]) * state[n] + part[row, :])
    return out, through + size


def nothing():
    zero = jnp.zeros((TILES, LANES), F32)
    return [zero] * NS, zero


def keep(out, state, through):
    for n in range(NS):
        out[n * TILES : (n + 1) * TILES, :] = state[n]
    out[NS * TILES :, :] = through


def join_body(shift, bits, *refs):
    place, rates, *rest = refs
    maps, rest = rest[: 1 << bits], rest[1 << bits :]
    before = rest[0] if len(rest) == 3 else None
    whole_out, before_out = rest[-2:]
    spot = (place[0] >> shift) & ((1 << bits) - 1)
    state, through = nothing()
    held_state, held_through = nothing()
    for k in range(1 << bits):
        here = spot == k
        held_state = [jnp.where(here, now, old) for now, old in zip(state, held_state)]
        held_through = jnp.where(here, through, held_through)
        part = maps[0][...]
        for distance in range(1, 1 << bits):
            part = jnp.where((spot ^ k) == distance, maps[distance][...], part)
        state, through = fold(rates, state, through, part)
    if len(whole_out.shape) == 3:
        even = parity_of(place) == 0
        for n in range(HALF):
            mine = jnp.where(even, state[n], state[n + HALF])
            for z in range(whole_out.shape[0]):
                whole_out[z, n * TILES : (n + 1) * TILES, :] = mine
        for z in range(whole_out.shape[0]):
            whole_out[z, HALF * TILES :, :] = through
    else:
        keep(whole_out, state, through)
    if before is not None:
        held_state, held_through = fold(rates, held_state, held_through, before)
    keep(before_out, held_state, held_through)


def join(place, rates, maps, before, shift, copies):
    bits = len(maps).bit_length() - 1
    one = jax.ShapeDtypeStruct(maps[0].shape, F32)
    halved = ((HALF + 1) * TILES, LANES)
    whole = jax.ShapeDtypeStruct((copies, *halved), F32) if copies else one
    given = [rates, *maps] + ([] if before is None else [before])
    body = functools.partial(join_body, shift, bits)
    estimate = cost(1 << 18, 1 << 19)
    return local(body, (whole, one), (), 1, len(given), estimate)(place, *given)


def planes_body(place, rates, planes, out):
    half = rates[pl.ds(pl.multiple_of(parity_of(place) * HALF * TILES, TILES), HALF * TILES), :]
    state = jnp.zeros((HALF * TILES, LANES), F32)
    for z in range(planes.shape[0]):
        size = jnp.concatenate([planes[z, HALF * TILES :, :]] * HALF, axis=0)
        later = jnp.exp2(size * half) * state + planes[z, : HALF * TILES, :]
        state = jnp.where(z < plane_of(place), later, state)
    out[...] = state


def join_planes(place, rates, planes):
    out = jax.ShapeDtypeStruct((HALF * TILES, LANES), F32)
    return local(planes_body, out, (), 1, 2, cost(1 << 18, 1 << 19))(place, rates, planes)


def final_body(
    place, low, proj, bias, xin, p0, p1, p2, p3, held, mine, theirs, before, gate, skip,
    out, wide, mix, steps, drive,
):
    rows = p0.shape[1]
    load_steps(low, proj, bias, xin, steps, drive)
    spread((p0, p1, p2, p3), 2 * NS, wide)
    rates = [held[n * TILES : (n + 1) * TILES, :] for n in range(NS)]
    even = parity_of(place) == 0
    rows_half = [slice(n * TILES, (n + 1) * TILES) for n in range(HALF)]
    state = [jnp.where(even, mine[row, :], theirs[row, :]) for row in rows_half]
    state += [jnp.where(even, theirs[row, :], mine[row, :]) for row in rows_half]
    _, through = nothing()
    state, _ = fold(held, state, through, before)

    def step(t, state):
        size, push = steps[rows_of(t), :], drive[rows_of(t), :]
        after = []
        result = None
        for n in range(NS):
            at = t * 2 * NS + n
            now = jnp.exp2(size * rates[n]) * state[n] + push * wide[pl.ds(at, 1), :]
            after.append(now)
            term = now * wide[pl.ds(at + NS, 1), :]
            result = term if result is None else result + term
        mix[rows_of(t), :] = result
        return tuple(after)

    lax.fori_loop(0, rows, step, tuple(state), unroll=4)
    for c in range(TILES):
        col = slice(c * LANES, (c + 1) * LANES)
        mixed = mix[pl.ds(c, rows, stride=TILES), :] + skip[:, col] * xin[:, col].astype(F32)
        opened = gate[:, col].astype(F32)
        out[:, col] = (mixed * (opened / (1.0 + jnp.exp(-opened)))).astype(BF16)


def finish(place, sources, partials, rates, halves, before, gate, skip):
    rows, width = gate.shape
    out = jax.ShapeDtypeStruct(gate.shape, BF16)
    tall = pltpu.VMEM((rows * TILES, LANES), F32)
    scratch = [pltpu.VMEM((rows * 2 * NS, LANES), F32), tall, tall, tall]
    estimate = cost(9 * rows * width * NS, 8 * rows * width, rows * width * NS)
    return local(final_body, out, scratch, 1, 14, estimate)(
        place, *sources, *partials, rates, *halves, before, gate, skip.reshape(1, -1)
    )


def exchange(x, groups):
    return lax.all_to_all(x, "ctx", 0, 0, axis_index_groups=groups, tiled=True)


def across(part, distance):
    count = lax.axis_size("ctx")
    return lax.ppermute(part, "ctx", [(i, i ^ distance) for i in range(count)])


def shards(query, key, value, xin, gate_z, w_bc, dt_low, dt_proj, dt_bias, a_rate, skip):
    ctx, tp = lax.axis_size("ctx"), lax.axis_size("tp")
    side, planes = 8, ctx // 16
    line = 2 * side
    index = lax.axis_index("ctx")
    place = index.astype(jnp.int32).reshape(1)
    along_y = [[z * line + 2 * y + c for y in range(side)] for z in range(planes) for c in (0, 1)]
    partner = [(i, i ^ 1) for i in range(ctx)]
    next_row = [(i, i + line) for i in range(ctx - line)]

    along_z = [[z * line + k for z in range(planes)] for k in range(line)]
    own = exchange(pack(key, value), along_y)
    queries = pack(query)
    own, queries = lax.optimization_barrier((own, queries))
    queries = exchange(queries, along_y)
    partial = project(xin, w_bc)
    partials = [partial] + [
        lax.ppermute(partial, "tp", [(i, (i + d) % tp) for i in range(tp)])
        for d in range(1, tp)
    ]
    sources = (dt_low, dt_proj, dt_bias.reshape(1, -1), xin)
    ends, rates = block_ends(sources, partials, a_rate)
    whole, before = join(place, rates, [ends, across(ends, 1)], None, 0, 0)
    maps = [whole] + [across(whole, 2 * d) for d in (1, 2, 3)]
    whole, before = join(place, rates, maps, before, 1, 0)
    whole, before = join(place, rates, [whole, across(whole, 8)], before, 3, planes)
    old_kv = lax.ppermute(own[side // 2 :], "ctx", next_row)
    wholes = exchange(whole, along_z)
    other = lax.ppermute(own, "ctx", partner)
    mine = join_planes(place, rates, wholes)
    theirs = across(mine, 1)
    past_kv = lax.ppermute(old_kv, "ctx", partner)
    later = attend_late(place, queries, own, other)
    attended = attend_early(place, queries, own, other, old_kv, past_kv, later)
    attended = exchange(attended, along_y)
    attended = unpack(attended)
    mixed = finish(place, sources, partials, rates, (mine, theirs), before, gate_z, skip)
    return (attended, mixed)


def solution(mesh):
    in_specs = (
        P("ctx", "tp"),
        P("ctx", "tp"),
        P("ctx", "tp"),
        P("ctx", "tp"),
        P("ctx", "tp"),
        P("tp", None),
        P("ctx", None),
        P(None, "tp"),
        P("tp"),
        P(None, "tp"),
        P("tp"),
    )
    out_specs = (P("ctx", "tp"), P("ctx", "tp"))
    return jax.shard_map(shards, mesh=mesh, in_specs=in_specs, out_specs=out_specs, check_vma=False)
```

```python
import functools

import jax
import jax.numpy as jnp
from jax import lax
from jax.experimental import pallas as pl
from jax.experimental.pallas import tpu as pltpu
from jax.sharding import PartitionSpec as P


HD = 128
WINDOW = 2048
NS = 16
HALF = NS // 2
LANES = 128
TILES = 8
LOG2E = 1.4426950408889634
F32 = jnp.float32
BF16 = jnp.bfloat16
VMEM = pl.BlockSpec(memory_space=pltpu.VMEM)
SMEM = pl.BlockSpec(memory_space=pltpu.SMEM)


def cost(flops, moved, exps=0):
    return pl.CostEstimate(flops=flops, bytes_accessed=moved, transcendentals=exps)


def local(body, outs, scratch=(), scalars=0, arrays=1, estimate=None, limit=20 << 20):
    return pl.pallas_call(
        body,
        out_shape=outs,
        in_specs=[SMEM] * scalars + [VMEM] * arrays,
        out_specs=jax.tree.map(lambda _: VMEM, outs),
        scratch_shapes=list(scratch),
        cost_estimate=estimate,
        compiler_params=pltpu.CompilerParams(vmem_limit_bytes=limit),
    )


def parity_of(place):
    return place[0] & 1


def plane_of(place):
    return place[0] >> 4


def pack_body(*refs):
    *ins, out, sems = refs
    rows = ins[0].shape[0]
    copies = []
    for head in range(out.shape[0]):
        for k, part in enumerate(ins):
            source = part.at[:, pl.ds(head * HD, HD)]
            target = out.at[head, pl.ds(k * rows, rows), :]
            copies.append(pltpu.make_async_copy(source, target, sems.at[head, k]))
    for copy in copies:
        copy.start()
    for copy in copies:
        copy.wait()


def pack(*parts):
    rows, width = parts[0].shape
    heads = width // HD
    return pl.pallas_call(
        pack_body,
        out_shape=jax.ShapeDtypeStruct((heads, len(parts) * rows, HD), BF16),
        in_specs=[pl.BlockSpec(memory_space=pl.ANY)] * len(parts),
        out_specs=VMEM,
        scratch_shapes=[pltpu.SemaphoreType.DMA((heads, len(parts)))],
        name="pack",
        cost_estimate=cost(0, 4 * len(parts) * rows * width),
    )(*parts)


def unpack_body(blocks, out):
    for head in range(blocks.shape[0]):
        out[:, head * HD : (head + 1) * HD] = blocks[head]


def unpack(blocks):
    heads, rows, _ = blocks.shape
    out = jax.ShapeDtypeStruct((rows, heads * HD), BF16)
    return local(unpack_body, out, estimate=cost(0, 4 * rows * heads * HD))(blocks)


def weigh(q, edge_pair, full, out, i):
    rows = q.shape[0]
    scale = HD**-0.5 * LOG2E
    columns = lax.broadcasted_iota(jnp.int32, (rows, rows), 1)
    below = columns <= lax.broadcasted_iota(jnp.int32, (rows, rows), 0)

    def dots(keys):
        return lax.dot_general(q, keys, (((1,), (1,)), ((), ())), preferred_element_type=F32)

    def gather(weights, values, ones):
        side = jnp.concatenate([values, ones], axis=1)
        return jnp.dot(weights, side, preferred_element_type=F32)

    (k_near, v_near, one_near), (k_far, v_far, one_far) = edge_pair
    scores = [jnp.where(below, dots(k_near), dots(k_far))] + [dots(k) for k, _, _ in full]
    top = None
    for part in scores:
        for c in range(0, rows, LANES):
            piece = part[:, c : c + LANES]
            top = piece if top is None else jnp.maximum(top, piece)
    top = jnp.max(top, axis=1, keepdims=True) * scale
    weights = [jnp.exp2(part * scale - top) for part in scores]
    total = gather(jnp.where(below, weights[0], 0.0).astype(BF16), v_near, one_near)
    total += gather(jnp.where(below, 0.0, weights[0]).astype(BF16), v_far, one_far)
    for part, (_, values, ones) in zip(weights[1:], full):
        total += gather(part.astype(BF16), values, ones)
    out[i] = (total[:, 0:HD] / total[:, HD : 2 * HD]).astype(BF16)


def late_body(place, own, other, out):
    half = out.shape[0]
    rows = out.shape[1]
    parity = parity_of(place)
    ones = jnp.ones((rows, HD), BF16)

    def block(source, b):
        return source[b, 0:rows, :], source[b, rows : 2 * rows, :], ones

    for i in range(half):
        full = [block(own, i + 1 + j) for j in range(half - 1)]
        full += [block(other, i + parity + j) for j in range(half)]
        weigh(own[half + i, 2 * rows :, :], (block(own, half + i), block(own, i)), full, out, i)


def early_body(place, own_far, other, old, past, later, out, ko, kp, own, sems):
    half, rows, _ = later.shape
    even = parity_of(place) == 0
    live = plane_of(place) > 0
    fetch = pltpu.make_async_copy(own_far.at[:half], own, sems.at[0])
    fetch.start()
    pass_on = pltpu.make_async_copy(later, out.at[half:], sems.at[1])
    pass_on.start()
    fetch.wait()
    key0 = jnp.where(even, own[0, 0:1, :].astype(F32), other[0, 0:1, :].astype(F32))
    key0 = jnp.broadcast_to(key0, (rows, HD)).astype(BF16)
    ones = jnp.ones((rows, HD), BF16)
    shown = jnp.where(live, jnp.ones((rows, HD), F32), jnp.zeros((rows, HD), F32)).astype(BF16)
    for keys, source in ((ko, old), (kp, past)):

        @pl.when(live)
        def _():
            for b in range(half):
                keys[b] = source[b, 0:rows, :]

        @pl.when(jnp.logical_not(live))
        def _():
            for b in range(half):
                keys[b] = key0

    def new(source, b):
        return source[b, 0:rows, :], source[b, rows : 2 * rows, :], ones

    def before(keys, source, b):
        return keys[b], source[b, rows : 2 * rows, :], shown

    def mine(b):
        return before(ko, old, b) if b < half else new(own, b - half)

    def either(first, second):
        return tuple(
            jnp.where(even, a.astype(F32), b.astype(F32)).astype(BF16) for a, b in zip(first, second)
        )

    def theirs(b):
        if b + 1 < half:
            at = b + parity_of(place)
            return kp[at], past[at, rows : 2 * rows, :], shown
        if b >= half:
            at = b - half + parity_of(place)
            return other[at, 0:rows, :], other[at, rows : 2 * rows, :], ones
        return either(before(kp, past, b), new(other, 0))

    for i in range(half):
        full = [mine(i + 1 + j) for j in range(half - 1)] + [theirs(i + j) for j in range(half)]
        weigh(own[i, 2 * rows :, :], (mine(half + i), mine(i)), full, out, i)
    pass_on.wait()


def attend_late(place, own, other):
    half, rows = own.shape[0] // 2, own.shape[1] // 3
    out = jax.ShapeDtypeStruct((half, rows, HD), BF16)
    estimate = cost(4 * half * rows * WINDOW * 2 * HD, 4 << 20, half * rows * WINDOW)
    return local(late_body, out, (), 1, 2, estimate)(place, own, other)


def attend_early(place, own, other, old, past, later):
    half, rows, _ = later.shape
    far = pl.BlockSpec(memory_space=pl.ANY)
    return pl.pallas_call(
        early_body,
        out_shape=jax.ShapeDtypeStruct((2 * half, rows, HD), BF16),
        in_specs=[SMEM, far, VMEM, VMEM, VMEM, far],
        out_specs=VMEM,
        scratch_shapes=[
            pltpu.VMEM((half, rows, HD), BF16),
            pltpu.VMEM((half, rows, HD), BF16),
            pltpu.VMEM((half, *own.shape[1:]), BF16),
            pltpu.SemaphoreType.DMA((2,)),
        ],
        name="early",
        cost_estimate=cost(4 * half * rows * WINDOW * 2 * HD, 4 << 20, half * rows * WINDOW),
        compiler_params=pltpu.CompilerParams(vmem_limit_bytes=63 << 20),
    )(place, own, other, old, past, later)


def rows_of(step):
    return pl.ds(pl.multiple_of(step * TILES, TILES), TILES)


def project_body(xin, w_bc, out):
    out[...] = jnp.dot(xin[...], w_bc[...], preferred_element_type=F32).T


def project(xin, w_bc):
    out = jax.ShapeDtypeStruct((w_bc.shape[1], xin.shape[0]), F32)
    return local(project_body, out, arrays=2, estimate=cost(0, 2 * xin.size))(xin, w_bc)


def load_steps(low, proj, bias, xin, steps, drive):
    rows = low.shape[0]
    for c in range(TILES):
        col = slice(c * LANES, (c + 1) * LANES)
        raw = jnp.dot(low[...], proj[:, col], preferred_element_type=F32) + bias[:, col]
        size = jnp.maximum(raw, 0.0) + jnp.log1p(jnp.exp(-jnp.abs(raw)))
        steps[pl.ds(c, rows, stride=TILES), :] = size
        drive[pl.ds(c, rows, stride=TILES), :] = size * xin[:, col].astype(F32)


def spread(parts, count, wide):
    total = parts[0][0:count, :]
    for part in parts[1:]:
        total = total + part[0:count, :]
    total = total.T
    rows = total.shape[0]
    for n in range(count):
        column = jnp.broadcast_to(total[:, n : n + 1], (rows, LANES))
        wide[pl.ds(n, rows, stride=count), :] = column


def load_rates(a_rate, held):
    for c in range(TILES):
        held[pl.ds(c, NS, stride=TILES), :] = a_rate[:, c * LANES : (c + 1) * LANES] * -LOG2E
    return [held[n * TILES : (n + 1) * TILES, :] for n in range(NS)]


def ends_body(low, proj, bias, xin, p0, p1, p2, p3, a_rate, out, held, wide, steps, drive):
    rows = p0.shape[1]
    load_steps(low, proj, bias, xin, steps, drive)
    spread((p0, p1, p2, p3), NS, wide)
    rates = load_rates(a_rate, held)

    def step(t, carry):
        state, through = carry
        size, push = steps[rows_of(t), :], drive[rows_of(t), :]
        state = tuple(
            jnp.exp2(size * rates[n]) * state[n] + push * wide[pl.ds(t * NS + n, 1), :]
            for n in range(NS)
        )
        return state, through + size

    zero = jnp.zeros((TILES, LANES), F32)
    state, through = lax.fori_loop(0, rows, step, ((zero,) * NS, zero), unroll=4)
    for n in range(NS):
        out[n * TILES : (n + 1) * TILES, :] = state[n]
    out[NS * TILES :, :] = through


def block_ends(sources, partials, a_rate):
    rows, width = sources[3].shape
    out = jax.ShapeDtypeStruct(((NS + 1) * TILES, LANES), F32)
    rates = jax.ShapeDtypeStruct((NS * TILES, LANES), F32)
    scratch = [pltpu.VMEM((rows * NS, LANES), F32)] + [pltpu.VMEM((rows * TILES, LANES), F32)] * 2
    estimate = cost(6 * rows * width * NS, 4 * rows * width, rows * width * NS)
    return local(ends_body, (out, rates), scratch, 0, 9, estimate)(*sources, *partials, a_rate)


def fold(rates, state, through, part):
    size = part[NS * TILES :, :]
    out = []
    for n in range(NS):
        row = slice(n * TILES, (n + 1) * TILES)
        out.append(jnp.exp2(size * rates[row, :]) * state[n] + part[row, :])
    return out, through + size


def nothing():
    zero = jnp.zeros((TILES, LANES), F32)
    return [zero] * NS, zero


def keep(out, state, through):
    for n in range(NS):
        out[n * TILES : (n + 1) * TILES, :] = state[n]
    out[NS * TILES :, :] = through


def join_body(shift, bits, *refs):
    place, rates, *rest = refs
    maps, rest = rest[: 1 << bits], rest[1 << bits :]
    before = rest[0] if len(rest) == 3 else None
    whole_out, before_out = rest[-2:]
    spot = (place[0] >> shift) & ((1 << bits) - 1)
    state, through = nothing()
    held_state, held_through = nothing()
    for k in range(1 << bits):
        here = spot == k
        held_state = [jnp.where(here, now, old) for now, old in zip(state, held_state)]
        held_through = jnp.where(here, through, held_through)
        part = maps[0][...]
        for distance in range(1, 1 << bits):
            part = jnp.where((spot ^ k) == distance, maps[distance][...], part)
        state, through = fold(rates, state, through, part)
    if len(whole_out.shape) == 3:
        even = parity_of(place) == 0
        for n in range(HALF):
            mine = jnp.where(even, state[n], state[n + HALF])
            for z in range(whole_out.shape[0]):
                whole_out[z, n * TILES : (n + 1) * TILES, :] = mine
        for z in range(whole_out.shape[0]):
            whole_out[z, HALF * TILES :, :] = through
    else:
        keep(whole_out, state, through)
    if before is not None:
        held_state, held_through = fold(rates, held_state, held_through, before)
    keep(before_out, held_state, held_through)


def join(place, rates, maps, before, shift, copies):
    bits = len(maps).bit_length() - 1
    one = jax.ShapeDtypeStruct(maps[0].shape, F32)
    halved = ((HALF + 1) * TILES, LANES)
    whole = jax.ShapeDtypeStruct((copies, *halved), F32) if copies else one
    given = [rates, *maps] + ([] if before is None else [before])
    body = functools.partial(join_body, shift, bits)
    estimate = cost(1 << 18, 1 << 19)
    return local(body, (whole, one), (), 1, len(given), estimate)(place, *given)


def planes_body(place, rates, planes, out):
    half = rates[pl.ds(pl.multiple_of(parity_of(place) * HALF * TILES, TILES), HALF * TILES), :]
    state = jnp.zeros((HALF * TILES, LANES), F32)
    for z in range(planes.shape[0]):
        size = jnp.concatenate([planes[z, HALF * TILES :, :]] * HALF, axis=0)
        later = jnp.exp2(size * half) * state + planes[z, : HALF * TILES, :]
        state = jnp.where(z < plane_of(place), later, state)
    out[...] = state


def join_planes(place, rates, planes):
    out = jax.ShapeDtypeStruct((HALF * TILES, LANES), F32)
    return local(planes_body, out, (), 1, 2, cost(1 << 18, 1 << 19))(place, rates, planes)


def final_body(
    place, low, proj, bias, xin, p0, p1, p2, p3, held, mine, theirs, before, gate, skip,
    out, wide, mix, steps, drive,
):
    rows = p0.shape[1]
    load_steps(low, proj, bias, xin, steps, drive)
    spread((p0, p1, p2, p3), 2 * NS, wide)
    rates = [held[n * TILES : (n + 1) * TILES, :] for n in range(NS)]
    even = parity_of(place) == 0
    rows_half = [slice(n * TILES, (n + 1) * TILES) for n in range(HALF)]
    state = [jnp.where(even, mine[row, :], theirs[row, :]) for row in rows_half]
    state += [jnp.where(even, theirs[row, :], mine[row, :]) for row in rows_half]
    _, through = nothing()
    state, _ = fold(held, state, through, before)

    def step(t, state):
        size, push = steps[rows_of(t), :], drive[rows_of(t), :]
        after = []
        result = None
        for n in range(NS):
            at = t * 2 * NS + n
            now = jnp.exp2(size * rates[n]) * state[n] + push * wide[pl.ds(at, 1), :]
            after.append(now)
            term = now * wide[pl.ds(at + NS, 1), :]
            result = term if result is None else result + term
        mix[rows_of(t), :] = result
        return tuple(after)

    lax.fori_loop(0, rows, step, tuple(state), unroll=4)
    for c in range(TILES):
        col = slice(c * LANES, (c + 1) * LANES)
        mixed = mix[pl.ds(c, rows, stride=TILES), :] + skip[:, col] * xin[:, col].astype(F32)
        opened = gate[:, col].astype(F32)
        out[:, col] = (mixed * (opened / (1.0 + jnp.exp(-opened)))).astype(BF16)


def finish(place, sources, partials, rates, halves, before, gate, skip):
    rows, width = gate.shape
    out = jax.ShapeDtypeStruct(gate.shape, BF16)
    tall = pltpu.VMEM((rows * TILES, LANES), F32)
    scratch = [pltpu.VMEM((rows * 2 * NS, LANES), F32), tall, tall, tall]
    estimate = cost(9 * rows * width * NS, 8 * rows * width, rows * width * NS)
    return local(final_body, out, scratch, 1, 14, estimate)(
        place, *sources, *partials, rates, *halves, before, gate, skip.reshape(1, -1)
    )


def exchange(x, groups):
    return lax.all_to_all(x, "ctx", 0, 0, axis_index_groups=groups, tiled=True)


def across(part, distance):
    count = lax.axis_size("ctx")
    return lax.ppermute(part, "ctx", [(i, i ^ distance) for i in range(count)])


def shards(query, key, value, xin, gate_z, w_bc, dt_low, dt_proj, dt_bias, a_rate, skip):
    ctx, tp = lax.axis_size("ctx"), lax.axis_size("tp")
    side, planes = 8, ctx // 16
    line = 2 * side
    index = lax.axis_index("ctx")
    place = index.astype(jnp.int32).reshape(1)
    along_y = [[z * line + 2 * y + c for y in range(side)] for z in range(planes) for c in (0, 1)]
    partner = [(i, i ^ 1) for i in range(ctx)]
    next_row = [(i, i + line) for i in range(ctx - line)]

    along_z = [[z * line + k for z in range(planes)] for k in range(line)]
    own = exchange(pack(key, value, query), along_y)
    partial = project(xin, w_bc)
    partials = [partial] + [
        lax.ppermute(partial, "tp", [(i, (i + d) % tp) for i in range(tp)])
        for d in range(1, tp)
    ]
    sources = (dt_low, dt_proj, dt_bias.reshape(1, -1), xin)
    ends, rates = block_ends(sources, partials, a_rate)
    whole, before = join(place, rates, [ends, across(ends, 1)], None, 0, 0)
    maps = [whole] + [across(whole, 2 * d) for d in (1, 2, 3)]
    whole, before = join(place, rates, maps, before, 1, 0)
    whole, before = join(place, rates, [whole, across(whole, 8)], before, 3, planes)
    old_kv = lax.ppermute(own[side // 2 :, : 2 * key.shape[0]], "ctx", next_row)
    wholes = exchange(whole, along_z)
    other = lax.ppermute(own, "ctx", partner)
    mine = join_planes(place, rates, wholes)
    theirs = across(mine, 1)
    past_kv = lax.ppermute(old_kv, "ctx", partner)
    later = attend_late(place, own, other)
    attended = attend_early(place, own, other, old_kv, past_kv, later)
    attended = exchange(attended, along_y)
    attended = unpack(attended)
    mixed = finish(place, sources, partials, rates, (mine, theirs), before, gate_z, skip)
    return (attended, mixed)


def solution(mesh):
    in_specs = (
        P("ctx", "tp"),
        P("ctx", "tp"),
        P("ctx", "tp"),
        P("ctx", "tp"),
        P("ctx", "tp"),
        P("tp", None),
        P("ctx", None),
        P(None, "tp"),
        P("tp"),
        P(None, "tp"),
        P("tp"),
    )
    out_specs = (P("ctx", "tp"), P("ctx", "tp"))
    return jax.shard_map(shards, mesh=mesh, in_specs=in_specs, out_specs=out_specs, check_vma=False)
```

```python
import functools

import jax
import jax.numpy as jnp
from jax import lax
from jax.experimental import pallas as pl
from jax.experimental.pallas import tpu as pltpu
from jax.sharding import PartitionSpec as P


HD = 128
WINDOW = 2048
NS = 16
HALF = NS // 2
LANES = 128
TILES = 8
LOG2E = 1.4426950408889634
F32 = jnp.float32
BF16 = jnp.bfloat16
VMEM = pl.BlockSpec(memory_space=pltpu.VMEM)
SMEM = pl.BlockSpec(memory_space=pltpu.SMEM)


def cost(flops, moved, exps=0):
    return pl.CostEstimate(flops=flops, bytes_accessed=moved, transcendentals=exps)


def local(body, outs, scratch=(), scalars=0, arrays=1, estimate=None, limit=20 << 20):
    return pl.pallas_call(
        body,
        out_shape=outs,
        in_specs=[SMEM] * scalars + [VMEM] * arrays,
        out_specs=jax.tree.map(lambda _: VMEM, outs),
        scratch_shapes=list(scratch),
        cost_estimate=estimate,
        compiler_params=pltpu.CompilerParams(vmem_limit_bytes=limit),
    )


def parity_of(place):
    return place[0] & 1


def plane_of(place):
    return place[0] >> 4


def pack_body(*refs):
    *ins, out, sems = refs
    rows = ins[0].shape[0]
    copies = []
    for head in range(out.shape[0]):
        for k, part in enumerate(ins):
            source = part.at[:, pl.ds(head * HD, HD)]
            target = out.at[head, pl.ds(k * rows, rows), :]
            copies.append(pltpu.make_async_copy(source, target, sems.at[head, k]))
    for copy in copies:
        copy.start()
    for copy in copies:
        copy.wait()


def pack(*parts):
    rows, width = parts[0].shape
    heads = width // HD
    return pl.pallas_call(
        pack_body,
        out_shape=jax.ShapeDtypeStruct((heads, len(parts) * rows, HD), BF16),
        in_specs=[pl.BlockSpec(memory_space=pl.ANY)] * len(parts),
        out_specs=VMEM,
        scratch_shapes=[pltpu.SemaphoreType.DMA((heads, len(parts)))],
        name="pack",
        cost_estimate=cost(0, 4 * len(parts) * rows * width),
    )(*parts)


def unpack_body(blocks, out):
    for head in range(blocks.shape[0]):
        out[:, head * HD : (head + 1) * HD] = blocks[head]


def unpack(blocks):
    heads, rows, _ = blocks.shape
    out = jax.ShapeDtypeStruct((rows, heads * HD), BF16)
    return local(unpack_body, out, estimate=cost(0, 4 * rows * heads * HD))(blocks)


def weigh(q, edge_pair, full, out, i):
    rows = q.shape[0]
    scale = HD**-0.5 * LOG2E
    columns = lax.broadcasted_iota(jnp.int32, (rows, rows), 1)
    below = columns <= lax.broadcasted_iota(jnp.int32, (rows, rows), 0)

    def dots(keys):
        return lax.dot_general(q, keys, (((1,), (1,)), ((), ())), preferred_element_type=F32)

    def gather(weights, values, ones):
        side = jnp.concatenate([values, ones], axis=1)
        return jnp.dot(weights, side, preferred_element_type=F32)

    (k_near, v_near, one_near), (k_far, v_far, one_far) = edge_pair
    scores = [jnp.where(below, dots(k_near), dots(k_far))] + [dots(k) for k, _, _ in full]
    top = None
    for part in scores:
        for c in range(0, rows, LANES):
            piece = part[:, c : c + LANES]
            top = piece if top is None else jnp.maximum(top, piece)
    top = jnp.max(top, axis=1, keepdims=True) * scale
    weights = [jnp.exp2(part * scale - top) for part in scores]
    total = gather(jnp.where(below, weights[0], 0.0).astype(BF16), v_near, one_near)
    total += gather(jnp.where(below, 0.0, weights[0]).astype(BF16), v_far, one_far)
    for part, (_, values, ones) in zip(weights[1:], full):
        total += gather(part.astype(BF16), values, ones)
    out[i] = (total[:, 0:HD] / total[:, HD : 2 * HD]).astype(BF16)


def late_body(place, own, other, out):
    half = out.shape[0]
    rows = out.shape[1]
    parity = parity_of(place)
    ones = jnp.ones((rows, HD), BF16)

    def block(source, b):
        return source[b, 0:rows, :], source[b, rows : 2 * rows, :], ones

    for i in range(half):
        full = [block(own, i + 1 + j) for j in range(half - 1)]
        full += [block(other, i + parity + j) for j in range(half)]
        weigh(own[half + i, 2 * rows :, :], (block(own, half + i), block(own, i)), full, out, i)


def early_body(place, own_far, other_far, old, past, later, out, ko, kp, own, other, sems):
    half, rows, _ = later.shape
    even = parity_of(place) == 0
    live = plane_of(place) > 0
    fetch = pltpu.make_async_copy(own_far.at[:half], own, sems.at[0])
    fetch.start()
    fetch_other = pltpu.make_async_copy(
        other_far.at[:half, pl.ds(0, 2 * rows), :], other, sems.at[2]
    )
    fetch_other.start()
    pass_on = pltpu.make_async_copy(later, out.at[half:], sems.at[1])
    pass_on.start()
    fetch.wait()
    fetch_other.wait()
    key0 = jnp.where(even, own[0, 0:1, :].astype(F32), other[0, 0:1, :].astype(F32))
    key0 = jnp.broadcast_to(key0, (rows, HD)).astype(BF16)
    ones = jnp.ones((rows, HD), BF16)
    shown = jnp.where(live, jnp.ones((rows, HD), F32), jnp.zeros((rows, HD), F32)).astype(BF16)
    for keys, source in ((ko, old), (kp, past)):

        @pl.when(live)
        def _():
            for b in range(half):
                keys[b] = source[b, 0:rows, :]

        @pl.when(jnp.logical_not(live))
        def _():
            for b in range(half):
                keys[b] = key0

    def new(source, b):
        return source[b, 0:rows, :], source[b, rows : 2 * rows, :], ones

    def before(keys, source, b):
        return keys[b], source[b, rows : 2 * rows, :], shown

    def mine(b):
        return before(ko, old, b) if b < half else new(own, b - half)

    def either(first, second):
        return tuple(
            jnp.where(even, a.astype(F32), b.astype(F32)).astype(BF16) for a, b in zip(first, second)
        )

    def theirs(b):
        if b + 1 < half:
            at = b + parity_of(place)
            return kp[at], past[at, rows : 2 * rows, :], shown
        if b >= half:
            at = b - half + parity_of(place)
            return other[at, 0:rows, :], other[at, rows : 2 * rows, :], ones
        return either(before(kp, past, b), new(other, 0))

    for i in range(half):
        full = [mine(i + 1 + j) for j in range(half - 1)] + [theirs(i + j) for j in range(half)]
        weigh(own[i, 2 * rows :, :], (mine(half + i), mine(i)), full, out, i)
    pass_on.wait()


def attend_late(place, own, other):
    half, rows = own.shape[0] // 2, own.shape[1] // 3
    out = jax.ShapeDtypeStruct((half, rows, HD), BF16)
    estimate = cost(4 * half * rows * WINDOW * 2 * HD, 4 << 20, half * rows * WINDOW)
    return local(late_body, out, (), 1, 2, estimate)(place, own, other)


def attend_early(place, own, other, old, past, later):
    half, rows, _ = later.shape
    far = pl.BlockSpec(memory_space=pl.ANY)
    return pl.pallas_call(
        early_body,
        out_shape=jax.ShapeDtypeStruct((2 * half, rows, HD), BF16),
        in_specs=[SMEM, far, far, VMEM, VMEM, far],
        out_specs=VMEM,
        scratch_shapes=[
            pltpu.VMEM((half, rows, HD), BF16),
            pltpu.VMEM((half, rows, HD), BF16),
            pltpu.VMEM((half, *own.shape[1:]), BF16),
            pltpu.VMEM((half, 2 * rows, HD), BF16),
            pltpu.SemaphoreType.DMA((3,)),
        ],
        name="early",
        cost_estimate=cost(4 * half * rows * WINDOW * 2 * HD, 4 << 20, half * rows * WINDOW),
        compiler_params=pltpu.CompilerParams(vmem_limit_bytes=63 << 20),
    )(place, own, other, old, past, later)


def rows_of(step):
    return pl.ds(pl.multiple_of(step * TILES, TILES), TILES)


def project_body(xin, w_bc, out):
    out[...] = jnp.dot(xin[...], w_bc[...], preferred_element_type=F32).T


def project(xin, w_bc):
    out = jax.ShapeDtypeStruct((w_bc.shape[1], xin.shape[0]), F32)
    return local(project_body, out, arrays=2, estimate=cost(0, 2 * xin.size))(xin, w_bc)


def load_steps(low, proj, bias, xin, steps, drive):
    rows = low.shape[0]
    for c in range(TILES):
        col = slice(c * LANES, (c + 1) * LANES)
        raw = jnp.dot(low[...], proj[:, col], preferred_element_type=F32) + bias[:, col]
        size = jnp.maximum(raw, 0.0) + jnp.log1p(jnp.exp(-jnp.abs(raw)))
        steps[pl.ds(c, rows, stride=TILES), :] = size
        drive[pl.ds(c, rows, stride=TILES), :] = size * xin[:, col].astype(F32)


def spread(parts, count, wide):
    total = parts[0][0:count, :]
    for part in parts[1:]:
        total = total + part[0:count, :]
    total = total.T
    rows = total.shape[0]
    for n in range(count):
        column = jnp.broadcast_to(total[:, n : n + 1], (rows, LANES))
        wide[pl.ds(n, rows, stride=count), :] = column


def load_rates(a_rate, held):
    for c in range(TILES):
        held[pl.ds(c, NS, stride=TILES), :] = a_rate[:, c * LANES : (c + 1) * LANES] * -LOG2E
    return [held[n * TILES : (n + 1) * TILES, :] for n in range(NS)]


def ends_body(low, proj, bias, xin, p0, p1, p2, p3, a_rate, out, held, wide, steps, drive):
    rows = p0.shape[1]
    load_steps(low, proj, bias, xin, steps, drive)
    spread((p0, p1, p2, p3), NS, wide)
    rates = load_rates(a_rate, held)

    def step(t, carry):
        state, through = carry
        size, push = steps[rows_of(t), :], drive[rows_of(t), :]
        state = tuple(
            jnp.exp2(size * rates[n]) * state[n] + push * wide[pl.ds(t * NS + n, 1), :]
            for n in range(NS)
        )
        return state, through + size

    zero = jnp.zeros((TILES, LANES), F32)
    state, through = lax.fori_loop(0, rows, step, ((zero,) * NS, zero), unroll=4)
    for n in range(NS):
        out[n * TILES : (n + 1) * TILES, :] = state[n]
    out[NS * TILES :, :] = through


def block_ends(sources, partials, a_rate):
    rows, width = sources[3].shape
    out = jax.ShapeDtypeStruct(((NS + 1) * TILES, LANES), F32)
    rates = jax.ShapeDtypeStruct((NS * TILES, LANES), F32)
    scratch = [pltpu.VMEM((rows * NS, LANES), F32)] + [pltpu.VMEM((rows * TILES, LANES), F32)] * 2
    estimate = cost(6 * rows * width * NS, 4 * rows * width, rows * width * NS)
    return local(ends_body, (out, rates), scratch, 0, 9, estimate)(*sources, *partials, a_rate)


def fold(rates, state, through, part):
    size = part[NS * TILES :, :]
    out = []
    for n in range(NS):
        row = slice(n * TILES, (n + 1) * TILES)
        out.append(jnp.exp2(size * rates[row, :]) * state[n] + part[row, :])
    return out, through + size


def nothing():
    zero = jnp.zeros((TILES, LANES), F32)
    return [zero] * NS, zero


def keep(out, state, through):
    for n in range(NS):
        out[n * TILES : (n + 1) * TILES, :] = state[n]
    out[NS * TILES :, :] = through


def join_body(shift, bits, *refs):
    place, rates, *rest = refs
    maps, rest = rest[: 1 << bits], rest[1 << bits :]
    before = rest[0] if len(rest) == 3 else None
    whole_out, before_out = rest[-2:]
    spot = (place[0] >> shift) & ((1 << bits) - 1)
    state, through = nothing()
    held_state, held_through = nothing()
    for k in range(1 << bits):
        here = spot == k
        held_state = [jnp.where(here, now, old) for now, old in zip(state, held_state)]
        held_through = jnp.where(here, through, held_through)
        part = maps[0][...]
        for distance in range(1, 1 << bits):
            part = jnp.where((spot ^ k) == distance, maps[distance][...], part)
        state, through = fold(rates, state, through, part)
    if len(whole_out.shape) == 3:
        even = parity_of(place) == 0
        for n in range(HALF):
            mine = jnp.where(even, state[n], state[n + HALF])
            for z in range(whole_out.shape[0]):
                whole_out[z, n * TILES : (n + 1) * TILES, :] = mine
        for z in range(whole_out.shape[0]):
            whole_out[z, HALF * TILES :, :] = through
    else:
        keep(whole_out, state, through)
    if before is not None:
        held_state, held_through = fold(rates, held_state, held_through, before)
    keep(before_out, held_state, held_through)


def join(place, rates, maps, before, shift, copies):
    bits = len(maps).bit_length() - 1
    one = jax.ShapeDtypeStruct(maps[0].shape, F32)
    halved = ((HALF + 1) * TILES, LANES)
    whole = jax.ShapeDtypeStruct((copies, *halved), F32) if copies else one
    given = [rates, *maps] + ([] if before is None else [before])
    body = functools.partial(join_body, shift, bits)
    estimate = cost(1 << 18, 1 << 19)
    return local(body, (whole, one), (), 1, len(given), estimate)(place, *given)


def planes_body(place, rates, planes, out):
    half = rates[pl.ds(pl.multiple_of(parity_of(place) * HALF * TILES, TILES), HALF * TILES), :]
    state = jnp.zeros((HALF * TILES, LANES), F32)
    for z in range(planes.shape[0]):
        size = jnp.concatenate([planes[z, HALF * TILES :, :]] * HALF, axis=0)
        later = jnp.exp2(size * half) * state + planes[z, : HALF * TILES, :]
        state = jnp.where(z < plane_of(place), later, state)
    out[...] = state


def join_planes(place, rates, planes):
    out = jax.ShapeDtypeStruct((HALF * TILES, LANES), F32)
    return local(planes_body, out, (), 1, 2, cost(1 << 18, 1 << 19))(place, rates, planes)


def final_body(
    place, low, proj, bias, xin, p0, p1, p2, p3, held, mine, theirs, before, gate, skip,
    out, wide, mix, steps, drive,
):
    rows = p0.shape[1]
    load_steps(low, proj, bias, xin, steps, drive)
    spread((p0, p1, p2, p3), 2 * NS, wide)
    rates = [held[n * TILES : (n + 1) * TILES, :] for n in range(NS)]
    even = parity_of(place) == 0
    rows_half = [slice(n * TILES, (n + 1) * TILES) for n in range(HALF)]
    state = [jnp.where(even, mine[row, :], theirs[row, :]) for row in rows_half]
    state += [jnp.where(even, theirs[row, :], mine[row, :]) for row in rows_half]
    _, through = nothing()
    state, _ = fold(held, state, through, before)

    def step(t, state):
        size, push = steps[rows_of(t), :], drive[rows_of(t), :]
        after = []
        result = None
        for n in range(NS):
            at = t * 2 * NS + n
            now = jnp.exp2(size * rates[n]) * state[n] + push * wide[pl.ds(at, 1), :]
            after.append(now)
            term = now * wide[pl.ds(at + NS, 1), :]
            result = term if result is None else result + term
        mix[rows_of(t), :] = result
        return tuple(after)

    lax.fori_loop(0, rows, step, tuple(state), unroll=4)
    for c in range(TILES):
        col = slice(c * LANES, (c + 1) * LANES)
        mixed = mix[pl.ds(c, rows, stride=TILES), :] + skip[:, col] * xin[:, col].astype(F32)
        opened = gate[:, col].astype(F32)
        out[:, col] = (mixed * (opened / (1.0 + jnp.exp(-opened)))).astype(BF16)


def finish(place, sources, partials, rates, halves, before, gate, skip):
    rows, width = gate.shape
    out = jax.ShapeDtypeStruct(gate.shape, BF16)
    tall = pltpu.VMEM((rows * TILES, LANES), F32)
    scratch = [pltpu.VMEM((rows * 2 * NS, LANES), F32), tall, tall, tall]
    estimate = cost(9 * rows * width * NS, 8 * rows * width, rows * width * NS)
    return local(final_body, out, scratch, 1, 14, estimate, 63 << 20)(
        place, *sources, *partials, rates, *halves, before, gate, skip.reshape(1, -1)
    )


def exchange(x, groups):
    return lax.all_to_all(x, "ctx", 0, 0, axis_index_groups=groups, tiled=True)


def across(part, distance):
    count = lax.axis_size("ctx")
    return lax.ppermute(part, "ctx", [(i, i ^ distance) for i in range(count)])


def shards(query, key, value, xin, gate_z, w_bc, dt_low, dt_proj, dt_bias, a_rate, skip):
    ctx, tp = lax.axis_size("ctx"), lax.axis_size("tp")
    side, planes = 8, ctx // 16
    line = 2 * side
    index = lax.axis_index("ctx")
    place = index.astype(jnp.int32).reshape(1)
    along_y = [[z * line + 2 * y + c for y in range(side)] for z in range(planes) for c in (0, 1)]
    partner = [(i, i ^ 1) for i in range(ctx)]
    next_row = [(i, i + line) for i in range(ctx - line)]

    along_z = [[z * line + k for z in range(planes)] for k in range(line)]
    own = exchange(pack(key, value, query), along_y)
    partial = project(xin, w_bc)
    partials = [partial] + [
        lax.ppermute(partial, "tp", [(i, (i + d) % tp) for i in range(tp)])
        for d in range(1, tp)
    ]
    sources = (dt_low, dt_proj, dt_bias.reshape(1, -1), xin)
    ends, rates = block_ends(sources, partials, a_rate)
    whole, before = join(place, rates, [ends, across(ends, 1)], None, 0, 0)
    maps = [whole] + [across(whole, 2 * d) for d in (1, 2, 3)]
    whole, before = join(place, rates, maps, before, 1, 0)
    whole, before = join(place, rates, [whole, across(whole, 8)], before, 3, planes)
    old_kv = lax.ppermute(own[side // 2 :, : 2 * key.shape[0]], "ctx", next_row)
    wholes = exchange(whole, along_z)
    other = lax.ppermute(own, "ctx", partner)
    mine = join_planes(place, rates, wholes)
    theirs = across(mine, 1)
    past_kv = lax.ppermute(old_kv, "ctx", partner)
    later = attend_late(place, own, other)
    attended = attend_early(place, own, other, old_kv, past_kv, later)
    attended = exchange(attended, along_y)
    attended = unpack(attended)
    mixed = finish(place, sources, partials, rates, (mine, theirs), before, gate_z, skip)
    return (attended, mixed)


def solution(mesh):
    in_specs = (
        P("ctx", "tp"),
        P("ctx", "tp"),
        P("ctx", "tp"),
        P("ctx", "tp"),
        P("ctx", "tp"),
        P("tp", None),
        P("ctx", None),
        P(None, "tp"),
        P("tp"),
        P(None, "tp"),
        P("tp"),
    )
    out_specs = (P("ctx", "tp"), P("ctx", "tp"))
    return jax.shard_map(shards, mesh=mesh, in_specs=in_specs, out_specs=out_specs, check_vma=False)
```
